32 devices in a mesh: group: 4 (over y, x), seq: 4 (over z), hid: 2 (over core).
Axes of the slice: x: 2, y: 2, z: 4, core: 2. Of those that a mesh axis runs over, the one named last changes fastest.
Arguments:
- tokens: bfloat16 [4, 8192, 1280], P('group', ('seq', 'hid')), may hold values from -6 to 6
- slot_embed: bfloat16 [1280, 16], replicated, may hold values from -6 to 6
- seq_lengths: int32 [4, 8], P('group'), may hold values from 1 to 2048, 8192 in all within a row
- w_in: bfloat16 [8, 1280, 2560], P(('seq', 'hid'), None, 'group'), may hold values from -0.3125 to 0.3125
- w_out: bfloat16 [8, 2560, 1280], P(('seq', 'hid'), 'group'), may hold values from -0.25 to 0.25
Outputs:
- mixed: bfloat16 [4, 8192, 1280], P('group', ('seq', 'hid'))
The draws below stay inside these ranges and needn't reach their ends.
Inputs may be any that keep to these rules, and one draw needn't show every extreme that they name: `seq_lengths`: each row sums to 8192; its largest entry is 2048.
All inputs are finite; a program needn't handle non-finite values.
Results may differ from the reference program's by a relative error of at most 0.013.
Values may be sent and summed in bfloat16 or wider, within the bound.
No kernel may reach another device: no remote copies, remote signals or barrier semaphores. Data moves between devices by JAX's collectives and lax.ppermute only.
A program may use at most 64 MiB of HBM per device.

```python
import math
import jax
import jax.numpy as jnp
import numpy as np
from jax import lax

D = 1280
HID = 2560
NSEQ = 8
EXPERTS = 8
SLOTS = 16
BATCHES = 4
PACK = 8192
MOST = 2048


def draw_tokens(key, part):
    main_key = jax.random.fold_in(key, 1)
    return jnp.clip(jax.random.normal(main_key, (BATCHES, PACK, D), jnp.float32), -6.0, 6.0).astype(jnp.bfloat16)


def draw_slot_embed(key, part):
    base_draw = jnp.clip(jax.random.normal(jax.random.fold_in(key, 5), (D, SLOTS), jnp.float32), -4.0, 4.0) * (2.5 / math.sqrt(D))
    return base_draw.astype(jnp.bfloat16)


def level_of(key, shape, pieces, smallest, top_value):
    gain = 1.0
    for axis_at, blocks in pieces:
        heights = jax.random.uniform(jax.random.fold_in(jax.random.fold_in(key, 6), axis_at), (blocks,), jnp.float32, smallest / len(pieces), top_value / len(pieces))
        gain = gain * jnp.repeat(jnp.exp(heights), shape[axis_at] // blocks).reshape((-1,) + (1,) * (len(shape) - 1 - axis_at))
    return gain


def profile(number_of, total, limit, skew):
    weights = [(1 << 20) // math.isqrt(rank ** skew) + 1 for rank in range(2, number_of + 1)]
    spare, holding = total - limit - (number_of - 1), [1] * (number_of - 1)
    while spare > 0:
        candidates = [i for i in range(number_of - 1) if holding[i] < limit]
        mass, budget = sum([weights[i] for i in candidates]), spare
        for i in candidates:
            extra = min(limit - holding[i], max(1, budget * weights[i] // mass), spare)
            holding[i] = holding[i] + extra
            spare = spare - extra
    return np.array([limit] + holding)


def uneven_parts(key, amount, total, bound, skew):
    if amount == 2:
        one = jax.random.randint(key, (), max(1, total - bound), min(bound, total - 1) + 1)
        return jnp.stack([one, total - one])
    tallies = jnp.asarray(profile(amount, total, bound, skew), jnp.int32)
    couples = (amount - 1) // 2
    donor, receiver = tallies[1:1 + 2 * couples:2], tallies[2:2 + 2 * couples:2]
    slack = jnp.minimum(donor - 1, bound - receiver)
    shifted = jax.random.randint(jax.random.fold_in(key, 1), (couples,), 0, 1 << 20) % (slack + 1)
    tallies = tallies.at[1:1 + 2 * couples:2].set(donor - shifted).at[2:2 + 2 * couples:2].set(receiver + shifted)
    return tallies[jax.random.permutation(jax.random.fold_in(key, 2), amount)]


def bell_draw(own_key, dims, deviation, bound, shards=(), held_as=jnp.bfloat16):
    gain = level_of(own_key, dims, shards, -0.22, 0.18) if shards else 1.0
    entries = jax.random.normal(own_key, dims, jnp.float32) * deviation * gain
    return jnp.minimum(jnp.maximum(entries, -bound), bound).astype(held_as)


def setup_inputs(seed: int = 0) -> dict:
    seeds = jax.random.split(jax.random.key(seed), 6)
    tokens = draw_tokens(jax.random.fold_in(seeds[5], 71), 0)
    slot_embed = draw_slot_embed(jax.random.fold_in(seeds[5], 71), 0)
    seq_lengths = jax.vmap(lambda own: uneven_parts(own, NSEQ, PACK, MOST, 2))(jax.random.split(seeds[2], BATCHES)).reshape((BATCHES, NSEQ)).astype(jnp.int32)
    w_in = bell_draw(seeds[3], (EXPERTS, D, HID), (D // 4) ** -0.5, 0.3125, ((0, 8), (2, 4)))
    w_out = bell_draw(seeds[4], (EXPERTS, HID, D), (HID // 4) ** -0.5, 0.25, ((0, 8), (1, 4)))
    return {"tokens": tokens, "slot_embed": slot_embed, "seq_lengths": seq_lengths, "w_in": w_in, "w_out": w_out}


def reference(tokens, slot_embed, seq_lengths, w_in, w_out):
    seq_end = jnp.cumsum(seq_lengths, axis=1).astype(jnp.int32)
    seq_start = (seq_end - seq_lengths).astype(jnp.int32)
    offsets = jnp.arange(MOST, dtype=jnp.int32)
    zero_index = jnp.zeros((), jnp.int32)

    def group_slots(inputs):
        group_rows, begins, sizes = inputs
        logits = jnp.dot(group_rows, slot_embed, preferred_element_type=jnp.float32)
        padded_logits = jnp.pad(logits, ((0, MOST), (0, 0)))
        padded_rows = jnp.pad(group_rows, ((0, MOST), (0, 0)))

        def dispatch_one(seq_inputs):
            seq_begin, seq_size = seq_inputs
            window_logits = lax.dynamic_slice(padded_logits, (seq_begin, zero_index), (MOST, SLOTS))
            row_block = lax.dynamic_slice(padded_rows, (seq_begin, zero_index), (MOST, D))
            inside = (offsets < seq_size)[:, None]
            column_max = jnp.max(jnp.where(inside, window_logits, -jnp.inf), axis=0)
            exponent = jnp.where(inside, jnp.exp(window_logits - column_max), 0.0)
            column_total = jnp.sum(exponent, axis=0)
            weights = (exponent / column_total).astype(jnp.bfloat16)
            return jnp.dot(weights.T, row_block, preferred_element_type=jnp.float32).astype(jnp.bfloat16)

        return lax.map(dispatch_one, (begins, sizes))

    slot_inputs = lax.map(group_slots, (tokens, seq_start, seq_lengths))

    def run_expert(expert_id):
        picked = lax.dynamic_slice_in_dim(slot_inputs, 2 * expert_id, 2, axis=2).reshape(-1, D)
        hidden = jax.nn.gelu(jnp.dot(picked, w_in[expert_id], preferred_element_type=jnp.float32), approximate=True).astype(jnp.bfloat16)
        result = jnp.dot(hidden, w_out[expert_id], preferred_element_type=jnp.float32).astype(jnp.bfloat16)
        return result.reshape(BATCHES, NSEQ, 2, D)

    expert_outputs = lax.map(run_expert, jnp.arange(EXPERTS, dtype=jnp.int32))
    slot_outputs = jnp.transpose(expert_outputs, (1, 2, 0, 3, 4)).reshape(BATCHES, NSEQ, SLOTS, D)

    def group_mix(inputs):
        group_rows, begins, sizes, group_slot_outputs = inputs
        logits = jnp.dot(group_rows, slot_embed, preferred_element_type=jnp.float32)
        mix_weights = jax.nn.softmax(logits, axis=1).astype(jnp.bfloat16)
        padded_mix = jnp.pad(mix_weights, ((0, MOST), (0, 0)))

        def add_sequence(running, seq_inputs):
            seq_begin, seq_size, slot_table = seq_inputs
            window_mix = lax.dynamic_slice(padded_mix, (seq_begin, zero_index), (MOST, SLOTS))
            contribution = jnp.dot(window_mix, slot_table, preferred_element_type=jnp.float32)
            inside = (offsets < seq_size)[:, None]
            current = lax.dynamic_slice(running, (seq_begin, zero_index), (MOST, D))
            running = lax.dynamic_update_slice(running, current + jnp.where(inside, contribution, 0.0), (seq_begin, zero_index))
            return running, None

        running = jnp.zeros((PACK + MOST, D), jnp.float32)
        running, _ = lax.scan(add_sequence, running, (begins, sizes, group_slot_outputs))
        return running[:PACK].astype(jnp.bfloat16)

    return lax.map(group_mix, (tokens, seq_start, seq_lengths, slot_outputs))
```

```python
import functools

import jax
import jax.numpy as jnp
from jax import lax
from jax.experimental import pallas as pl
from jax.experimental.pallas import tpu as pltpu
from jax.sharding import PartitionSpec as P


EMPTY = -1e30
STAT = 128
BF16 = jnp.bfloat16
F32 = jnp.float32
VMEM = pl.BlockSpec(memory_space=pltpu.VMEM)
SMEM = pl.BlockSpec(memory_space=pltpu.SMEM)
ANY = pl.BlockSpec(memory_space=pl.ANY)


def partner(index, step, size):
    if size & (size - 1) == 0:
        return index ^ step
    return (index + step) % size


def source(index, step, size):
    if size & (size - 1) == 0:
        return index ^ step
    return (index - step) % size


def swap(value, axis, step):
    size = lax.axis_size(axis)
    return lax.ppermute(value, axis, [(i, partner(i, step, size)) for i in range(size)])


def split3(value):
    high = value.astype(BF16)
    rest = value - high.astype(F32)
    mid = rest.astype(BF16)
    low = (rest - mid.astype(F32)).astype(BF16)
    return high.astype(F32), mid.astype(F32), low.astype(F32)


def pack_stats(peak, total):
    rows = peak.shape[0]
    lane = lax.broadcasted_iota(jnp.int32, (rows, STAT), 1)
    out = jnp.zeros((rows, STAT), F32)
    for at, part in enumerate(split3(peak) + split3(total)):
        out = jnp.where(lane == at, part, out)
    return out.astype(BF16)


def read_stats(block):
    stats = block.astype(F32)
    lane = lax.broadcasted_iota(jnp.int32, stats.shape, 1)
    peak = jnp.sum(jnp.where(lane < 3, stats, 0.0), axis=1, keepdims=True)
    total = jnp.sum(jnp.where((lane >= 3) & (lane < 6), stats, 0.0), axis=1, keepdims=True)
    return peak, total


def member_mask(lengths_ref, offset, seq_count, tok_count):
    row = lax.broadcasted_iota(jnp.int32, (seq_count, tok_count), 0)
    place = offset + lax.broadcasted_iota(jnp.int32, (seq_count, tok_count), 1)
    begin = jnp.int32(0)
    starts = jnp.zeros((seq_count, tok_count), jnp.int32)
    ends = jnp.zeros((seq_count, tok_count), jnp.int32)
    for s in range(seq_count):
        end = begin + lengths_ref[s]
        starts = jnp.where(row == s, begin, starts)
        ends = jnp.where(row == s, end, ends)
        begin = end
    return (place >= starts) & (place < ends)


def local_kernel(cfg, where_ref, lengths_ref, embed_ref, tok_hbm, *refs):
    outs, logits_ref = refs[: cfg["hid"]], refs[cfg["hid"]]
    tok_ref, weight_ref, peak_ref, total_ref, sems = refs[cfg["hid"] + 1 :]
    tok_count, width = tok_ref.shape
    seq_count, per = cfg["seqs"], cfg["per"]
    rows = per * seq_count
    chunk = tok_count // cfg["chunks"]
    copies = []
    for i in range(cfg["chunks"]):
        part = pl.ds(i * chunk, chunk)
        copy = pltpu.make_async_copy(tok_hbm.at[0, part], tok_ref.at[part], sems.at[i])
        copy.start()
        copies.append(copy)
    mask = member_mask(lengths_ref, where_ref[2], seq_count, tok_count)
    for i in range(cfg["chunks"]):
        copies[i].wait()
        part = pl.ds(i * chunk, chunk)
        logits_ref[:, part] = lax.dot_general(
            embed_ref[...],
            tok_ref[part, :],
            (((1,), (1,)), ((), ())),
            preferred_element_type=F32,
        )
    place = 0
    for u in range(cfg["hid"]):
        for k in range(cfg["seq"]):
            expert = partner(where_ref[0], k, cfg["seq"]) * cfg["hid"] + partner(
                where_ref[1], u, cfg["hid"]
            )
            parts, peaks, totals = [], [], []
            for i in range(per):
                row = logits_ref[pl.ds(expert * per + i, 1), :]
                masked = jnp.where(mask, row, EMPTY)
                peak = jnp.max(masked, axis=1, keepdims=True)
                exponent = jnp.where(mask, jnp.exp(masked - peak), 0.0)
                parts.append(exponent)
                peaks.append(peak)
                totals.append(jnp.sum(exponent, axis=1, keepdims=True))
            here = pl.ds(place * rows, rows)
            weight_ref[here, :] = jnp.concatenate(parts, axis=0).astype(BF16)
            peak_ref[here, :] = jnp.concatenate(peaks, axis=0)
            total_ref[here, :] = jnp.concatenate(totals, axis=0)
            place += 1
    each = cfg["seq"] * rows
    for u in range(cfg["hid"]):
        here = pl.ds(u * each, each)
        sums = jnp.dot(weight_ref[here, :], tok_ref[...], preferred_element_type=F32)
        total = total_ref[here, :]
        outs[u][:, :width] = (sums / jnp.maximum(total, 1.0)).astype(BF16)
        outs[u][:, width:] = pack_stats(peak_ref[here, :], total)


def merge_blocks(blocks, width):
    stats = [read_stats(b[:, width:]) for b in blocks]
    peak = functools.reduce(jnp.maximum, [s[0] for s in stats])
    weights = [s[1] * jnp.exp(s[0] - peak) for s in stats]
    total = sum(weights)
    inverse = 1.0 / jnp.maximum(total, 1.0)
    merged = sum(b[:, :width].astype(F32) * (w * inverse) for b, w in zip(blocks, weights))
    return merged.astype(BF16), peak, total


def chip_kernel(count, *refs):
    ins, outs = refs[:count], refs[count:]
    rows, wide = outs[0].shape
    width = wide - STAT
    for k, out in enumerate(outs):
        here = slice(k * rows, (k + 1) * rows)
        merged, peak, total = merge_blocks([r[here, :] for r in ins], width)
        out[:, :width] = merged
        out[:, width:] = pack_stats(peak, total)


def column_kernel(*refs):
    ins, out = refs[:-1], refs[-1]
    merged, _, _ = merge_blocks([r[...] for r in ins], out.shape[1])
    out[...] = merged


def expert_kernel(count, *refs):
    ins, (w_in_ref, w_out_ref), outs = refs[:count], refs[count : count + 2], refs[count + 2 :]
    rows = ins[0].shape[0]
    picked = jnp.concatenate([r[...] for r in ins], axis=0)
    hidden = jax.nn.gelu(
        jnp.dot(picked, w_in_ref[0], preferred_element_type=F32), approximate=True
    ).astype(BF16)
    result = jnp.dot(hidden, w_out_ref[0], preferred_element_type=F32).astype(BF16)
    for k, out in enumerate(outs):
        out[...] = result[k * rows : (k + 1) * rows, :]


def table_kernel(cfg, where_ref, lengths_ref, logits_ref, table_ref, mix_ref, wide_ref):
    slot_count, tok_count = logits_ref.shape
    seq_count, per = cfg["seqs"], cfg["per"]
    rows = per * seq_count
    logits = logits_ref[...]
    raised = jnp.exp(logits - jnp.max(logits, axis=0, keepdims=True))
    mix_ref[...] = raised / jnp.sum(raised, axis=0, keepdims=True)
    mask = member_mask(lengths_ref, where_ref[2], seq_count, tok_count)
    place = 0
    for u in range(cfg["hid"]):
        for k in range(cfg["seq"]):
            expert = source(where_ref[0], k, cfg["seq"]) * cfg["hid"] + source(
                where_ref[1], u, cfg["hid"]
            )
            parts = [
                jnp.where(mask, mix_ref[pl.ds(expert * per + i, 1), :], 0.0) for i in range(per)
            ]
            wide_ref[pl.ds(place * rows, rows), :] = jnp.concatenate(parts, axis=0)
            place += 1
    table_ref[...] = jnp.transpose(wide_ref[...], (1, 0)).astype(BF16)


def mix_kernel(count, table_ref, *refs):
    ins, out, held = refs[:count], refs[count], refs[count + 1]
    rows = ins[0].shape[0]

    @pl.when(pl.program_id(0) == 0)
    def _():
        for k, r in enumerate(ins):
            held[k * rows : (k + 1) * rows, :] = r[...]

    out[0] = jnp.dot(table_ref[...], held[...], preferred_element_type=F32).astype(BF16)


def body(tokens, slot_embed, seq_lengths, w_in, w_out):
    _, tok_count, width = tokens.shape
    slot_count = slot_embed.shape[1]
    seq_count = seq_lengths.shape[1]
    groups, columns, cores = (lax.axis_size(a) for a in ("group", "seq", "hid"))
    per = slot_count // (columns * cores)
    rows = per * seq_count
    all_rows = slot_count * seq_count
    cfg = dict(hid=cores, seq=columns, seqs=seq_count, per=per, chunks=4)
    column, core = lax.axis_index("seq"), lax.axis_index("hid")
    where = jnp.stack([column, core, (column * cores + core) * tok_count]).astype(jnp.int32)
    lengths = seq_lengths[0]

    outs = pl.pallas_call(
        functools.partial(local_kernel, cfg),
        out_shape=[jax.ShapeDtypeStruct((columns * rows, width + STAT), BF16)] * cores
        + [jax.ShapeDtypeStruct((slot_count, tok_count), F32)],
        in_specs=[SMEM, SMEM, VMEM, ANY],
        out_specs=[VMEM] * (cores + 1),
        scratch_shapes=[
            pltpu.VMEM((tok_count, width), BF16),
            pltpu.VMEM((all_rows, tok_count), BF16),
            pltpu.VMEM((all_rows, 1), F32),
            pltpu.VMEM((all_rows, 1), F32),
            pltpu.SemaphoreType.DMA((cfg["chunks"],)),
        ],
        name="local",
    )(where, lengths, slot_embed.T, tokens)
    sums, logits = outs[:cores], outs[cores]

    table = pl.pallas_call(
        functools.partial(table_kernel, cfg),
        out_shape=jax.ShapeDtypeStruct((tok_count, all_rows), BF16),
        in_specs=[SMEM, SMEM, VMEM],
        out_specs=VMEM,
        scratch_shapes=[
            pltpu.VMEM((slot_count, tok_count), F32),
            pltpu.VMEM((all_rows, tok_count), F32),
        ],
        cost_estimate=pl.CostEstimate(
            flops=8 * all_rows * tok_count, bytes_accessed=4 * all_rows * tok_count, transcendentals=slot_count * tok_count
        ),
        name="table",
    )(where, lengths, logits)

    chip = [sums[0]] + [swap(sums[u], "hid", u) for u in range(1, cores)]
    blocks = pl.pallas_call(
        functools.partial(chip_kernel, cores),
        out_shape=[jax.ShapeDtypeStruct((rows, width + STAT), BF16)] * columns,
        in_specs=[VMEM] * cores,
        out_specs=[VMEM] * columns,
        name="chip",
    )(*chip)

    got = [blocks[0]] + [swap(blocks[k], "seq", k) for k in range(1, columns)]
    own = pl.pallas_call(
        column_kernel,
        out_shape=jax.ShapeDtypeStruct((rows, width), BF16),
        in_specs=[VMEM] * columns,
        out_specs=VMEM,
        name="column",
    )(*got)

    spread = [own] + [swap(own, "group", k) for k in range(1, groups)]
    parts = pl.pallas_call(
        functools.partial(expert_kernel, groups),
        out_shape=[jax.ShapeDtypeStruct((rows, width), BF16)] * groups,
        in_specs=[VMEM] * (groups + 2),
        out_specs=[VMEM] * groups,
        name="expert",
    )(*spread, w_in, w_out)
    back = [parts[0]] + [
        swap(parts[k], "group", k if groups & (groups - 1) == 0 else groups - k)
        for k in range(1, groups)
    ]
    slot_rows = sum(b.astype(F32) for b in back).astype(BF16)

    column_rows = [slot_rows] + [swap(slot_rows, "seq", k) for k in range(1, columns)]
    every = list(column_rows)
    for u in range(1, cores):
        every += [swap(r, "hid", u) for r in column_rows]

    tile = tok_count // 4
    return pl.pallas_call(
        functools.partial(mix_kernel, len(every)),
        grid=(4,),
        out_shape=jax.ShapeDtypeStruct((1, tok_count, width), BF16),
        in_specs=[pl.BlockSpec((tile, all_rows), lambda i: (i, 0))] + [VMEM] * len(every),
        out_specs=pl.BlockSpec((1, tile, width), lambda i: (0, i, 0)),
        scratch_shapes=[pltpu.VMEM((all_rows, width), BF16)],
        name="mix",
    )(table, *every)


def solution(mesh):
    placed = (
        P("group", ("seq", "hid"), None),
        P(),
        P("group", None),
        P(("seq", "hid"), None, "group"),
        P(("seq", "hid"), "group", None),
    )
    return jax.shard_map(
        body,
        mesh=mesh,
        in_specs=placed,
        out_specs=P("group", ("seq", "hid"), None),
        check_vma=False,
    )
```

```python
import functools

import jax
import jax.numpy as jnp
from jax import lax
from jax.experimental import pallas as pl
from jax.experimental.pallas import tpu as pltpu
from jax.sharding import PartitionSpec as P


CHIP_VMEM = 67043328
EMPTY = -1e30
STAT = 128
BF16 = jnp.bfloat16
F32 = jnp.float32
VMEM = pl.BlockSpec(memory_space=pltpu.VMEM)
SMEM = pl.BlockSpec(memory_space=pltpu.SMEM)
HBM = pl.BlockSpec(memory_space=pltpu.HBM)


def params(*arrays):
    size = sum(2 * count * each for count, each in arrays)
    return pltpu.CompilerParams(vmem_limit_bytes=int(size) + (4 << 20))


def partner(index, step, size):
    if size & (size - 1) == 0:
        return index ^ step
    return (index + step) % size


def source(index, step, size):
    if size & (size - 1) == 0:
        return index ^ step
    return (index - step) % size


def swap(value, axis, step):
    size = lax.axis_size(axis)
    return lax.ppermute(value, axis, [(i, partner(i, step, size)) for i in range(size)])


def split3(value):
    high = value.astype(BF16)
    rest = value - high.astype(F32)
    mid = rest.astype(BF16)
    low = (rest - mid.astype(F32)).astype(BF16)
    return high.astype(F32), mid.astype(F32), low.astype(F32)


def pack_stats(peak, total):
    rows = peak.shape[0]
    lane = lax.broadcasted_iota(jnp.int32, (rows, STAT), 1)
    out = jnp.zeros((rows, STAT), F32)
    for at, part in enumerate(split3(peak) + split3(total)):
        out = jnp.where(lane == at, part, out)
    return out.astype(BF16)


def read_stats(block):
    stats = block.astype(F32)
    lane = lax.broadcasted_iota(jnp.int32, stats.shape, 1)
    peak = jnp.sum(jnp.where(lane < 3, stats, 0.0), axis=1, keepdims=True)
    total = jnp.sum(jnp.where((lane >= 3) & (lane < 6), stats, 0.0), axis=1, keepdims=True)
    return peak, total


def member_mask(lengths_ref, offset, seq_count, tok_count):
    row = lax.broadcasted_iota(jnp.int32, (seq_count, tok_count), 0)
    place = offset + lax.broadcasted_iota(jnp.int32, (seq_count, tok_count), 1)
    begin = jnp.int32(0)
    starts = jnp.zeros((seq_count, tok_count), jnp.int32)
    ends = jnp.zeros((seq_count, tok_count), jnp.int32)
    for s in range(seq_count):
        end = begin + lengths_ref[0, s]
        starts = jnp.where(row == s, begin, starts)
        ends = jnp.where(row == s, end, ends)
        begin = end
    return (place >= starts) & (place < ends)


def place_of(cfg, tok_count):
    column, core = lax.axis_index("seq"), lax.axis_index("hid")
    return column, core, (column * cfg["hid"] + core) * tok_count


def local_kernel(cfg, lengths_hbm, embed_hbm, tok_hbm, *refs):
    outs, logits_ref = refs[: cfg["hid"]], refs[cfg["hid"]]
    (tok_ref, embed_ref, lengths_ref, weight_ref, peak_ref, total_ref, sems, small) = refs[
        cfg["hid"] + 1 :
    ]
    tok_count, width = tok_ref.shape
    seq_count, per = cfg["seqs"], cfg["per"]
    rows = per * seq_count
    chunk = tok_count // cfg["chunks"]
    get_embed = pltpu.make_async_copy(embed_hbm, embed_ref, small.at[0])
    get_embed.start()
    get_lengths = pltpu.make_async_copy(lengths_hbm, lengths_ref, small.at[1])
    get_lengths.start()
    copies = []
    for i in range(cfg["chunks"]):
        part = pl.ds(i * chunk, chunk)
        copy = pltpu.make_async_copy(tok_hbm.at[0, part], tok_ref.at[part], sems.at[i])
        copy.start()
        copies.append(copy)
    column, core, offset = place_of(cfg, tok_count)
    get_lengths.wait()
    mask = member_mask(lengths_ref, offset, seq_count, tok_count)
    get_embed.wait()
    for i in range(cfg["chunks"]):
        copies[i].wait()
        part = pl.ds(i * chunk, chunk)
        logits_ref[:, part] = lax.dot_general(
            embed_ref[...],
            tok_ref[part, :],
            (((1,), (1,)), ((), ())),
            preferred_element_type=F32,
        )
    place = 0
    for u in range(cfg["hid"]):
        for k in range(cfg["seq"]):
            expert = partner(column, k, cfg["seq"]) * cfg["hid"] + partner(core, u, cfg["hid"])
            parts, peaks, totals = [], [], []
            for i in range(per):
                row = logits_ref[pl.ds(expert * per + i, 1), :]
                masked = jnp.where(mask, row, EMPTY)
                peak = jnp.max(masked, axis=1, keepdims=True)
                exponent = jnp.where(mask, jnp.exp(masked - peak), 0.0)
                parts.append(exponent)
                peaks.append(peak)
                totals.append(jnp.sum(exponent, axis=1, keepdims=True))
            here = pl.ds(place * rows, rows)
            weight_ref[here, :] = jnp.concatenate(parts, axis=0).astype(BF16)
            peak_ref[here, :] = jnp.concatenate(peaks, axis=0)
            total_ref[here, :] = jnp.concatenate(totals, axis=0)
            place += 1
    each = cfg["seq"] * rows
    for u in range(cfg["hid"]):
        here = pl.ds(u * each, each)
        sums = jnp.dot(weight_ref[here, :], tok_ref[...], preferred_element_type=F32)
        total = total_ref[here, :]
        outs[u][:, :width] = (sums / jnp.maximum(total, 1.0)).astype(BF16)
        outs[u][:, width:] = pack_stats(peak_ref[here, :], total)


def merge_blocks(blocks, width):
    stats = [read_stats(b[:, width:]) for b in blocks]
    peak = functools.reduce(jnp.maximum, [s[0] for s in stats])
    weights = [s[1] * jnp.exp(s[0] - peak) for s in stats]
    total = sum(weights)
    inverse = 1.0 / jnp.maximum(total, 1.0)
    merged = sum(b[:, :width].astype(F32) * (w * inverse) for b, w in zip(blocks, weights))
    return merged.astype(BF16), peak, total


def chip_kernel(count, *refs):
    ins, outs = refs[:count], refs[count:]
    rows, wide = outs[0].shape
    width = wide - STAT
    for k, out in enumerate(outs):
        here = slice(k * rows, (k + 1) * rows)
        merged, peak, total = merge_blocks([r[here, :] for r in ins], width)
        out[:, :width] = merged
        out[:, width:] = pack_stats(peak, total)


def column_kernel(*refs):
    ins, out = refs[:-4], refs[-1]
    merged, _, _ = merge_blocks([r[...] for r in ins], out.shape[1])
    out[...] = merged


def expert_kernel(count, *refs):
    ins, (w_in_ref, w_out_ref), outs = refs[:count], refs[count : count + 2], refs[count + 2 :]
    rows = ins[0].shape[0]
    picked = jnp.concatenate([r[...] for r in ins], axis=0)
    hidden = jax.nn.gelu(
        jnp.dot(picked, w_in_ref[0], preferred_element_type=F32), approximate=True
    ).astype(BF16)
    result = jnp.dot(hidden, w_out_ref[0], preferred_element_type=F32).astype(BF16)
    for k, out in enumerate(outs):
        out[...] = result[k * rows : (k + 1) * rows, :]


def table_kernel(cfg, lengths_ref, logits_ref, table_ref, mix_ref, wide_ref):
    slot_count, tok_count = logits_ref.shape
    seq_count, per = cfg["seqs"], cfg["per"]
    rows = per * seq_count
    logits = logits_ref[...]
    raised = jnp.exp(logits - jnp.max(logits, axis=0, keepdims=True))
    mix_ref[...] = raised / jnp.sum(raised, axis=0, keepdims=True)
    column, core, offset = place_of(cfg, tok_count)
    mask = member_mask(lengths_ref, offset, seq_count, tok_count)
    place = 0
    for u in range(cfg["hid"]):
        for k in range(cfg["seq"]):
            expert = source(column, k, cfg["seq"]) * cfg["hid"] + source(core, u, cfg["hid"])
            parts = [
                jnp.where(mask, mix_ref[pl.ds(expert * per + i, 1), :], 0.0) for i in range(per)
            ]
            wide_ref[pl.ds(place * rows, rows), :] = jnp.concatenate(parts, axis=0)
            place += 1
    table_ref[...] = jnp.transpose(wide_ref[...], (1, 0)).astype(BF16)


def mix_kernel(count, table_ref, *refs):
    ins, out, held = refs[:count], refs[count], refs[count + 1]
    rows = ins[0].shape[0]

    @pl.when(pl.program_id(0) == 0)
    def _():
        for k, r in enumerate(ins):
            held[k * rows : (k + 1) * rows, :] = r[...]

    out[0] = jnp.dot(table_ref[...], held[...], preferred_element_type=F32).astype(BF16)


def body(tokens, slot_embed, seq_lengths, w_in, w_out):
    _, tok_count, width = tokens.shape
    slot_count = slot_embed.shape[1]
    seq_count = seq_lengths.shape[1]
    groups, columns, cores = (lax.axis_size(a) for a in ("group", "seq", "hid"))
    per = slot_count // (columns * cores)
    rows = per * seq_count
    all_rows = slot_count * seq_count
    cfg = dict(hid=cores, seq=columns, seqs=seq_count, per=per, chunks=4)

    outs = pl.pallas_call(
        functools.partial(local_kernel, cfg),
        out_shape=[jax.ShapeDtypeStruct((columns * rows, width + STAT), BF16)] * cores
        + [jax.ShapeDtypeStruct((slot_count, tok_count), F32)],
        in_specs=[HBM, HBM, HBM],
        out_specs=[VMEM] * (cores + 1),
        scratch_shapes=[
            pltpu.VMEM((tok_count, width), BF16),
            pltpu.VMEM((slot_count, width), BF16),
            pltpu.SMEM((1, seq_count), jnp.int32),
            pltpu.VMEM((all_rows, tok_count), BF16),
            pltpu.VMEM((all_rows, 1), F32),
            pltpu.VMEM((all_rows, 1), F32),
            pltpu.SemaphoreType.DMA((cfg["chunks"],)),
            pltpu.SemaphoreType.DMA((2,)),
        ],
        compiler_params=params((tok_count * width, 2), (all_rows * tok_count, 4), (all_rows * width, 6)),
        name="local",
    )(*(pltpu.with_memory_space_constraint(v, pltpu.HBM) for v in (seq_lengths, slot_embed.T, tokens)))
    sums, logits = outs[:cores], outs[cores]

    table = pl.pallas_call(
        functools.partial(table_kernel, cfg),
        out_shape=jax.ShapeDtypeStruct((tok_count, all_rows), BF16),
        in_specs=[SMEM, VMEM],
        out_specs=VMEM,
        scratch_shapes=[
            pltpu.VMEM((slot_count, tok_count), F32),
            pltpu.VMEM((all_rows, tok_count), F32),
        ],
        cost_estimate=pl.CostEstimate(
            flops=8 * all_rows * tok_count, bytes_accessed=4 * all_rows * tok_count, transcendentals=slot_count * tok_count
        ),
        compiler_params=params((all_rows * tok_count, 8)),
        name="table",
    )(seq_lengths, logits)

    chip = [sums[0]] + [swap(sums[u], "hid", u) for u in range(1, cores)]
    blocks = pl.pallas_call(
        functools.partial(chip_kernel, cores),
        out_shape=[jax.ShapeDtypeStruct((rows, width + STAT), BF16)] * columns,
        in_specs=[VMEM] * cores,
        out_specs=[VMEM] * columns,
        compiler_params=params((all_rows * width, 6)),
        name="chip",
    )(*chip)

    got = [blocks[0]] + [swap(blocks[k], "seq", k) for k in range(1, columns)]
    own = pl.pallas_call(
        column_kernel,
        out_shape=jax.ShapeDtypeStruct((rows, width), BF16),
        in_specs=[VMEM] * (columns + 3),
        out_specs=VMEM,
        compiler_params=params((all_rows * width, 6)),
        name="column",
    )(*got, table, w_in, w_out)

    spread = [own] + [swap(own, "group", k) for k in range(1, groups)]
    parts = pl.pallas_call(
        functools.partial(expert_kernel, groups),
        out_shape=[jax.ShapeDtypeStruct((rows, width), BF16)] * groups,
        in_specs=[VMEM] * (groups + 2),
        out_specs=[VMEM] * groups,
        compiler_params=params((w_in.size, 2), (w_out.size, 2), (groups * rows * width, 6)),
        name="expert",
    )(*spread, w_in, w_out)
    back = [parts[0]] + [
        swap(parts[k], "group", k if groups & (groups - 1) == 0 else groups - k)
        for k in range(1, groups)
    ]
    slot_rows = sum(b.astype(F32) for b in back).astype(BF16)

    column_rows = [slot_rows] + [swap(slot_rows, "seq", k) for k in range(1, columns)]
    every = list(column_rows)
    for u in range(1, cores):
        every += [swap(r, "hid", u) for r in column_rows]

    tile = tok_count // 4
    return pl.pallas_call(
        functools.partial(mix_kernel, len(every)),
        grid=(4,),
        out_shape=jax.ShapeDtypeStruct((1, tok_count, width), BF16),
        in_specs=[pl.BlockSpec((tile, all_rows), lambda i: (i, 0))] + [VMEM] * len(every),
        out_specs=pl.BlockSpec((1, tile, width), lambda i: (0, i, 0)),
        scratch_shapes=[pltpu.VMEM((all_rows, width), BF16)],
        compiler_params=params((all_rows * width, 4), (tok_count * width, 4)),
        name="mix",
    )(table, *every)


def solution(mesh):
    placed = (
        P("group", ("seq", "hid"), None),
        P(),
        P("group", None),
        P(("seq", "hid"), None, "group"),
        P(("seq", "hid"), "group", None),
    )
    return jax.shard_map(
        body,
        mesh=mesh,
        in_specs=placed,
        out_specs=P("group", ("seq", "hid"), None),
        check_vma=False,
    )
```

```python
import functools

import jax
import jax.numpy as jnp
from jax import lax
from jax.experimental import pallas as pl
from jax.experimental.pallas import tpu as pltpu
from jax.sharding import PartitionSpec as P


CHIP_VMEM = 67043328
EMPTY = -1e30
STAT = 128
BF16 = jnp.bfloat16
F32 = jnp.float32
VMEM = pl.BlockSpec(memory_space=pltpu.VMEM)
SMEM = pl.BlockSpec(memory_space=pltpu.SMEM)
HBM = pl.BlockSpec(memory_space=pltpu.HBM)


def params(*arrays):
    size = sum(2 * count * each for count, each in arrays)
    return pltpu.CompilerParams(vmem_limit_bytes=int(size) + (4 << 20))


def partner(index, step, size):
    if size & (size - 1) == 0:
        return index ^ step
    return (index + step) % size


def far_first(size):
    return [0] + list(range(size - 1, 0, -1))


def source(index, step, size):
    if size & (size - 1) == 0:
        return index ^ step
    return (index - step) % size


def far(value):
    return pltpu.with_memory_space_constraint(value, pltpu.HBM)


def swap(value, axis, step):
    size = lax.axis_size(axis)
    return lax.ppermute(value, axis, [(i, partner(i, step, size)) for i in range(size)])


def split3(value):
    high = value.astype(BF16)
    rest = value - high.astype(F32)
    mid = rest.astype(BF16)
    low = (rest - mid.astype(F32)).astype(BF16)
    return high.astype(F32), mid.astype(F32), low.astype(F32)


def pack_stats(peak, total):
    rows = peak.shape[0]
    lane = lax.broadcasted_iota(jnp.int32, (rows, STAT), 1)
    out = jnp.zeros((rows, STAT), F32)
    for at, part in enumerate(split3(peak) + split3(total)):
        out = jnp.where(lane == at, part, out)
    return out.astype(BF16)


def read_stats(block):
    stats = block.astype(F32)
    lane = lax.broadcasted_iota(jnp.int32, stats.shape, 1)
    peak = jnp.sum(jnp.where(lane < 3, stats, 0.0), axis=1, keepdims=True)
    total = jnp.sum(jnp.where((lane >= 3) & (lane < 6), stats, 0.0), axis=1, keepdims=True)
    return peak, total


def member_mask(lengths_ref, offset, seq_count, tok_count):
    row = lax.broadcasted_iota(jnp.int32, (seq_count, tok_count), 0)
    place = offset + lax.broadcasted_iota(jnp.int32, (seq_count, tok_count), 1)
    begin = jnp.int32(0)
    starts = jnp.zeros((seq_count, tok_count), jnp.int32)
    ends = jnp.zeros((seq_count, tok_count), jnp.int32)
    for s in range(seq_count):
        end = begin + lengths_ref[0, s]
        starts = jnp.where(row == s, begin, starts)
        ends = jnp.where(row == s, end, ends)
        begin = end
    return (place >= starts) & (place < ends)


def place_of(cfg, tok_count):
    column, core = lax.axis_index("seq"), lax.axis_index("hid")
    return column, core, (column * cfg["hid"] + core) * tok_count


def local_kernel(cfg, lengths_hbm, embed_hbm, tok_hbm, *refs):
    outs, logits_ref = refs[: cfg["hid"]], refs[cfg["hid"]]
    (tok_ref, embed_ref, lengths_ref, weight_ref, peak_ref, total_ref, sems, small) = refs[
        cfg["hid"] + 1 :
    ]
    tok_count, width = tok_ref.shape
    seq_count, per = cfg["seqs"], cfg["per"]
    rows = per * seq_count
    chunk = tok_count // cfg["chunks"]
    get_embed = pltpu.make_async_copy(embed_hbm, embed_ref, small.at[0])
    get_embed.start()
    get_lengths = pltpu.make_async_copy(lengths_hbm, lengths_ref, small.at[1])
    get_lengths.start()
    copies = []
    for i in range(cfg["chunks"]):
        part = pl.ds(i * chunk, chunk)
        copy = pltpu.make_async_copy(tok_hbm.at[0, part], tok_ref.at[part], sems.at[i])
        copy.start()
        copies.append(copy)
    column, core, offset = place_of(cfg, tok_count)
    get_lengths.wait()
    mask = member_mask(lengths_ref, offset, seq_count, tok_count)
    get_embed.wait()
    for i in range(cfg["chunks"]):
        copies[i].wait()
        part = pl.ds(i * chunk, chunk)
        logits_ref[:, part] = lax.dot_general(
            embed_ref[...],
            tok_ref[part, :],
            (((1,), (1,)), ((), ())),
            preferred_element_type=F32,
        )
    place = 0
    for u in range(cfg["hid"]):
        for k in range(cfg["seq"]):
            expert = partner(column, k, cfg["seq"]) * cfg["hid"] + partner(core, u, cfg["hid"])
            parts, peaks, totals = [], [], []
            for i in range(per):
                row = logits_ref[pl.ds(expert * per + i, 1), :]
                masked = jnp.where(mask, row, EMPTY)
                peak = jnp.max(masked, axis=1, keepdims=True)
                exponent = jnp.where(mask, jnp.exp(masked - peak), 0.0)
                parts.append(exponent)
                peaks.append(peak)
                totals.append(jnp.sum(exponent, axis=1, keepdims=True))
            here = pl.ds(place * rows, rows)
            weight_ref[here, :] = jnp.concatenate(parts, axis=0).astype(BF16)
            peak_ref[here, :] = jnp.concatenate(peaks, axis=0)
            total_ref[here, :] = jnp.concatenate(totals, axis=0)
            place += 1
    each = cfg["seq"] * rows
    full = jnp.dot(weight_ref[...], tok_ref[...], preferred_element_type=F32)
    for u in range(cfg["hid"]):
        here = pl.ds(u * each, each)
        sums = full[u * each : (u + 1) * each]
        total = total_ref[here, :]
        outs[u][:, :width] = (sums / jnp.maximum(total, 1.0)).astype(BF16)
        outs[u][:, width:] = pack_stats(peak_ref[here, :], total)


def merge_blocks(blocks, width):
    stats = [read_stats(b[:, width:]) for b in blocks]
    peak = functools.reduce(jnp.maximum, [s[0] for s in stats])
    weights = [s[1] * jnp.exp(s[0] - peak) for s in stats]
    total = sum(weights)
    inverse = 1.0 / jnp.maximum(total, 1.0)
    merged = sum(b[:, :width].astype(F32) * (w * inverse) for b, w in zip(blocks, weights))
    return merged.astype(BF16), peak, total


def chip_kernel(count, *refs):
    ins, outs = refs[:count], refs[count:]
    rows, wide = outs[0].shape
    width = wide - STAT
    for k, out in zip(far_first(len(outs)), outs):
        here = slice(k * rows, (k + 1) * rows)
        merged, peak, total = merge_blocks([r[here, :] for r in ins], width)
        out[:, :width] = merged
        out[:, width:] = pack_stats(peak, total)


def column_kernel(*refs):
    ins, out = refs[:-2], refs[-1]
    merged, _, _ = merge_blocks([r[...] for r in ins], out.shape[1])
    out[...] = merged


def expert_kernel(count, *refs):
    ins, (w_in_ref, w_out_ref), outs = refs[:count], refs[count : count + 2], refs[count + 2 :]
    rows = ins[0].shape[0]
    picked = jnp.concatenate([r[...] for r in ins], axis=0)
    hidden = jax.nn.gelu(
        jnp.dot(picked, w_in_ref[0], preferred_element_type=F32), approximate=True
    ).astype(BF16)
    result = jnp.dot(hidden, w_out_ref[0], preferred_element_type=F32).astype(BF16)
    for k, out in zip(far_first(len(outs)), outs):
        out[...] = result[k * rows : (k + 1) * rows, :]


def table_kernel(cfg, lengths_ref, logits_ref, *refs):
    loads, (table_ref, *kept), (mix_ref, wide_ref, sems) = refs[:2], refs[2:5], refs[5:]
    copies = [pltpu.make_async_copy(a, b, sems.at[i]) for i, (a, b) in enumerate(zip(loads, kept))]
    for copy in copies:
        copy.start()
    slot_count, tok_count = logits_ref.shape
    seq_count, per = cfg["seqs"], cfg["per"]
    rows = per * seq_count
    logits = logits_ref[...]
    raised = jnp.exp(logits - jnp.max(logits, axis=0, keepdims=True))
    mix_ref[...] = raised / jnp.sum(raised, axis=0, keepdims=True)
    column, core, offset = place_of(cfg, tok_count)
    mask = member_mask(lengths_ref, offset, seq_count, tok_count)
    place = 0
    for u in range(cfg["hid"]):
        for k in range(cfg["seq"]):
            expert = source(column, k, cfg["seq"]) * cfg["hid"] + source(core, u, cfg["hid"])
            parts = [
                jnp.where(mask, mix_ref[pl.ds(expert * per + i, 1), :], 0.0) for i in range(per)
            ]
            wide_ref[pl.ds(place * rows, rows), :] = jnp.concatenate(parts, axis=0)
            place += 1
    table_ref[...] = jnp.transpose(wide_ref[...], (1, 0)).astype(BF16)
    for copy in copies:
        copy.wait()


def mix_kernel(count, table_ref, *refs):
    ins, out, held = refs[:count], refs[count], refs[count + 1]
    rows = ins[0].shape[0]
    done, sems = refs[count + 2 :]
    for k, r in enumerate(ins):
        held[k * rows : (k + 1) * rows, :] = r[...]
    steps = sems.shape[0]
    tile = table_ref.shape[0] // steps
    copies = []
    for i in range(steps):
        part = pl.ds(i * tile, tile)
        done[part, :] = jnp.dot(table_ref[part, :], held[...], preferred_element_type=F32).astype(BF16)
        copy = pltpu.make_async_copy(done.at[part], out.at[0, part], sems.at[i])
        copy.start()
        copies.append(copy)
    for copy in copies:
        copy.wait()


def body(tokens, slot_embed, seq_lengths, w_in, w_out):
    _, tok_count, width = tokens.shape
    slot_count = slot_embed.shape[1]
    seq_count = seq_lengths.shape[1]
    groups, columns, cores = (lax.axis_size(a) for a in ("group", "seq", "hid"))
    per = slot_count // (columns * cores)
    rows = per * seq_count
    all_rows = slot_count * seq_count
    cfg = dict(hid=cores, seq=columns, seqs=seq_count, per=per, chunks=2)

    outs = pl.pallas_call(
        functools.partial(local_kernel, cfg),
        out_shape=[jax.ShapeDtypeStruct((columns * rows, width + STAT), BF16)] * cores
        + [jax.ShapeDtypeStruct((slot_count, tok_count), F32)],
        in_specs=[HBM, HBM, HBM],
        out_specs=[VMEM] * (cores + 1),
        scratch_shapes=[
            pltpu.VMEM((tok_count, width), BF16),
            pltpu.VMEM((slot_count, width), BF16),
            pltpu.SMEM((1, seq_count), jnp.int32),
            pltpu.VMEM((all_rows, tok_count), BF16),
            pltpu.VMEM((all_rows, 1), F32),
            pltpu.VMEM((all_rows, 1), F32),
            pltpu.SemaphoreType.DMA((cfg["chunks"],)),
            pltpu.SemaphoreType.DMA((2,)),
        ],
        compiler_params=params((tok_count * width, 2), (all_rows * tok_count, 4), (all_rows * width, 6)),
        name="local",
    )(far(seq_lengths), far(slot_embed.T), far(tokens))
    sums, logits = outs[:cores], outs[cores]

    table, near_in, near_out = pl.pallas_call(
        functools.partial(table_kernel, cfg),
        out_shape=[
            jax.ShapeDtypeStruct((tok_count, all_rows), BF16),
            jax.ShapeDtypeStruct(w_in.shape, BF16),
            jax.ShapeDtypeStruct(w_out.shape, BF16),
        ],
        in_specs=[SMEM, VMEM, HBM, HBM],
        out_specs=[VMEM] * 3,
        scratch_shapes=[
            pltpu.VMEM((slot_count, tok_count), F32),
            pltpu.VMEM((all_rows, tok_count), F32),
            pltpu.SemaphoreType.DMA((2,)),
        ],
        cost_estimate=pl.CostEstimate(
            flops=8 * all_rows * tok_count, bytes_accessed=4 * all_rows * tok_count, transcendentals=slot_count * tok_count
        ),
        compiler_params=params((all_rows * tok_count, 8), (w_in.size, 4)),
        name="table",
    )(seq_lengths, logits, far(w_in), far(w_out))

    chip = [sums[0]] + [swap(sums[u], "hid", u) for u in range(1, cores)]
    blocks = pl.pallas_call(
        functools.partial(chip_kernel, cores),
        out_shape=[jax.ShapeDtypeStruct((rows, width + STAT), BF16)] * columns,
        in_specs=[VMEM] * cores,
        out_specs=[VMEM] * columns,
        compiler_params=params((all_rows * width, 6)),
        name="chip",
    )(*chip)

    got = [blocks[0]] + [swap(b, "seq", k) for k, b in zip(far_first(columns), blocks) if k]
    own = pl.pallas_call(
        column_kernel,
        out_shape=jax.ShapeDtypeStruct((rows, width), BF16),
        in_specs=[VMEM] * (columns + 1),
        out_specs=VMEM,
        compiler_params=params((all_rows * width, 6)),
        name="column",
    )(*got, table)

    spread = [own] + [swap(own, "group", k) for k in range(1, groups)]
    parts = pl.pallas_call(
        functools.partial(expert_kernel, groups),
        out_shape=[jax.ShapeDtypeStruct((rows, width), BF16)] * groups,
        in_specs=[VMEM] * (groups + 2),
        out_specs=[VMEM] * groups,
        compiler_params=params((w_in.size, 2), (w_out.size, 2), (groups * rows * width, 6)),
        name="expert",
    )(*spread, near_in, near_out)
    back = [parts[0]] + [
        swap(part, "group", k if groups & (groups - 1) == 0 else groups - k)
        for k, part in zip(far_first(groups), parts)
        if k
    ]
    slot_rows = sum(b.astype(F32) for b in back).astype(BF16)

    column_rows = [slot_rows] + [swap(slot_rows, "seq", k) for k in range(1, columns)]
    every = list(column_rows)
    for u in range(1, cores):
        every += [swap(r, "hid", u) for r in column_rows]

    return pl.pallas_call(
        functools.partial(mix_kernel, len(every)),
        out_shape=jax.ShapeDtypeStruct((1, tok_count, width), BF16),
        in_specs=[VMEM] * (1 + len(every)),
        out_specs=HBM,
        scratch_shapes=[
            pltpu.VMEM((all_rows, width), BF16),
            pltpu.VMEM((tok_count, width), BF16),
            pltpu.SemaphoreType.DMA((8,)),
        ],
        compiler_params=params((all_rows * width, 4), (tok_count * width, 4)),
        name="mix",
    )(table, *every)


def solution(mesh):
    placed = (
        P("group", ("seq", "hid"), None),
        P(),
        P("group", None),
        P(("seq", "hid"), None, "group"),
        P(("seq", "hid"), "group", None),
    )
    return jax.shard_map(
        body,
        mesh=mesh,
        in_specs=placed,
        out_specs=P("group", ("seq", "hid"), None),
        check_vma=False,
    )
```

```python
import functools

import jax
import jax.numpy as jnp
from jax import lax
from jax.experimental import pallas as pl
from jax.experimental.pallas import tpu as pltpu
from jax.sharding import PartitionSpec as P


CHIP_VMEM = 67043328
EMPTY = -1e30
STAT = 128
BF16 = jnp.bfloat16
F32 = jnp.float32
VMEM = pl.BlockSpec(memory_space=pltpu.VMEM)
SMEM = pl.BlockSpec(memory_space=pltpu.SMEM)
HBM = pl.BlockSpec(memory_space=pltpu.HBM)


def params(*arrays):
    size = sum(2 * count * each for count, each in arrays)
    return pltpu.CompilerParams(vmem_limit_bytes=int(size) + (4 << 20))


def partner(index, step, size):
    if size & (size - 1) == 0:
        return index ^ step
    return (index + step) % size


def far_first(size):
    return [0] + list(range(size - 1, 0, -1))


def source(index, step, size):
    if size & (size - 1) == 0:
        return index ^ step
    return (index - step) % size


def far(value):
    return pltpu.with_memory_space_constraint(value, pltpu.HBM)


def swap(value, axis, step):
    size = lax.axis_size(axis)
    return lax.ppermute(value, axis, [(i, partner(i, step, size)) for i in range(size)])


def mirror(core, cores):
    return cores - 1 - core


def cross(value, axis, step):
    size, cores = lax.axis_size(axis), lax.axis_size("hid")
    pairs = [
        (i * cores + c, partner(i, step, size) * cores + mirror(c, cores))
        for i in range(size)
        for c in range(cores)
    ]
    return lax.ppermute(value, (axis, "hid"), pairs)


def reflect(value):
    cores = lax.axis_size("hid")
    return lax.ppermute(value, "hid", [(c, mirror(c, cores)) for c in range(cores)])


def expert_of(column, core, step, cfg):
    return column * cfg["hid"] + (core if step else mirror(core, cfg["hid"]))


def split3(value):
    high = value.astype(BF16)
    rest = value - high.astype(F32)
    mid = rest.astype(BF16)
    low = (rest - mid.astype(F32)).astype(BF16)
    return high.astype(F32), mid.astype(F32), low.astype(F32)


def pack_stats(peak, total):
    rows = peak.shape[0]
    lane = lax.broadcasted_iota(jnp.int32, (rows, STAT), 1)
    out = jnp.zeros((rows, STAT), F32)
    for at, part in enumerate(split3(peak) + split3(total)):
        out = jnp.where(lane == at, part, out)
    return out.astype(BF16)


def read_stats(block):
    stats = block.astype(F32)
    lane = lax.broadcasted_iota(jnp.int32, stats.shape, 1)
    peak = jnp.sum(jnp.where(lane < 3, stats, 0.0), axis=1, keepdims=True)
    total = jnp.sum(jnp.where((lane >= 3) & (lane < 6), stats, 0.0), axis=1, keepdims=True)
    return peak, total


def member_mask(lengths_ref, offset, seq_count, tok_count):
    row = lax.broadcasted_iota(jnp.int32, (seq_count, tok_count), 0)
    place = offset + lax.broadcasted_iota(jnp.int32, (seq_count, tok_count), 1)
    begin = jnp.int32(0)
    starts = jnp.zeros((seq_count, tok_count), jnp.int32)
    ends = jnp.zeros((seq_count, tok_count), jnp.int32)
    for s in range(seq_count):
        end = begin + lengths_ref[0, s]
        starts = jnp.where(row == s, begin, starts)
        ends = jnp.where(row == s, end, ends)
        begin = end
    return (place >= starts) & (place < ends)


def place_of(cfg, tok_count):
    column, core = lax.axis_index("seq"), lax.axis_index("hid")
    return column, core, (column * cfg["hid"] + core) * tok_count


def local_kernel(cfg, lengths_hbm, embed_hbm, tok_hbm, *refs):
    outs, logits_ref = refs[: cfg["hid"]], refs[cfg["hid"]]
    (tok_ref, embed_ref, lengths_ref, weight_ref, peak_ref, total_ref, sems, small) = refs[
        cfg["hid"] + 1 :
    ]
    tok_count, width = tok_ref.shape
    seq_count, per = cfg["seqs"], cfg["per"]
    rows = per * seq_count
    chunk = tok_count // cfg["chunks"]
    get_embed = pltpu.make_async_copy(embed_hbm, embed_ref, small.at[0])
    get_embed.start()
    get_lengths = pltpu.make_async_copy(lengths_hbm, lengths_ref, small.at[1])
    get_lengths.start()
    copies = []
    for i in range(cfg["chunks"]):
        part = pl.ds(i * chunk, chunk)
        copy = pltpu.make_async_copy(tok_hbm.at[0, part], tok_ref.at[part], sems.at[i])
        copy.start()
        copies.append(copy)
    column, core, offset = place_of(cfg, tok_count)
    get_lengths.wait()
    mask = member_mask(lengths_ref, offset, seq_count, tok_count)
    get_embed.wait()
    for i in range(cfg["chunks"]):
        copies[i].wait()
        part = pl.ds(i * chunk, chunk)
        logits_ref[:, part] = lax.dot_general(
            embed_ref[...],
            tok_ref[part, :],
            (((1,), (1,)), ((), ())),
            preferred_element_type=F32,
        )
    place = 0
    for u in range(cfg["hid"]):
        for k in range(cfg["seq"]):
            expert = expert_of(partner(column, k, cfg["seq"]), partner(core, u, cfg["hid"]), k, cfg)
            parts, peaks, totals = [], [], []
            for i in range(per):
                row = logits_ref[pl.ds(expert * per + i, 1), :]
                masked = jnp.where(mask, row, EMPTY)
                peak = jnp.max(masked, axis=1, keepdims=True)
                exponent = jnp.where(mask, jnp.exp(masked - peak), 0.0)
                parts.append(exponent)
                peaks.append(peak)
                totals.append(jnp.sum(exponent, axis=1, keepdims=True))
            here = pl.ds(place * rows, rows)
            weight_ref[here, :] = jnp.concatenate(parts, axis=0).astype(BF16)
            peak_ref[here, :] = jnp.concatenate(peaks, axis=0)
            total_ref[here, :] = jnp.concatenate(totals, axis=0)
            place += 1
    each = cfg["seq"] * rows
    full = jnp.dot(weight_ref[...], tok_ref[...], preferred_element_type=F32)
    for u in range(cfg["hid"]):
        here = pl.ds(u * each, each)
        sums = full[u * each : (u + 1) * each]
        total = total_ref[here, :]
        outs[u][:, :width] = (sums / jnp.maximum(total, 1.0)).astype(BF16)
        outs[u][:, width:] = pack_stats(peak_ref[here, :], total)


def merge_blocks(blocks, width):
    stats = [read_stats(b[:, width:]) for b in blocks]
    peak = functools.reduce(jnp.maximum, [s[0] for s in stats])
    weights = [s[1] * jnp.exp(s[0] - peak) for s in stats]
    total = sum(weights)
    inverse = 1.0 / jnp.maximum(total, 1.0)
    merged = sum(b[:, :width].astype(F32) * (w * inverse) for b, w in zip(blocks, weights))
    return merged.astype(BF16), peak, total


def chip_kernel(count, *refs):
    ins, outs = refs[:count], refs[count:]
    rows, wide = outs[0].shape
    width = wide - STAT
    for k, out in zip(far_first(len(outs)), outs):
        here = slice(k * rows, (k + 1) * rows)
        merged, peak, total = merge_blocks([r[here, :] for r in ins], width)
        out[:, :width] = merged
        out[:, width:] = pack_stats(peak, total)


def column_kernel(*refs):
    ins, out = refs[:-2], refs[-1]
    merged, _, _ = merge_blocks([r[...] for r in ins], out.shape[1])
    out[...] = merged


def expert_kernel(count, *refs):
    ins, (w_in_ref, w_out_ref), outs = refs[:count], refs[count : count + 2], refs[count + 2 :]
    rows = ins[0].shape[0]
    picked = jnp.concatenate([r[...] for r in ins], axis=0)
    hidden = jax.nn.gelu(
        jnp.dot(picked, w_in_ref[0], preferred_element_type=F32), approximate=True
    ).astype(BF16)
    result = jnp.dot(hidden, w_out_ref[0], preferred_element_type=F32).astype(BF16)
    for k, out in zip(far_first(len(outs)), outs):
        out[...] = result[k * rows : (k + 1) * rows, :]


def table_kernel(cfg, lengths_ref, logits_ref, *refs):
    loads, (table_ref, *kept), (mix_ref, wide_ref, sems) = refs[:2], refs[2:5], refs[5:]
    copies = [pltpu.make_async_copy(a, b, sems.at[i]) for i, (a, b) in enumerate(zip(loads, kept))]
    for copy in copies:
        copy.start()
    slot_count, tok_count = logits_ref.shape
    seq_count, per = cfg["seqs"], cfg["per"]
    rows = per * seq_count
    logits = logits_ref[...]
    raised = jnp.exp(logits - jnp.max(logits, axis=0, keepdims=True))
    mix_ref[...] = raised / jnp.sum(raised, axis=0, keepdims=True)
    column, core, offset = place_of(cfg, tok_count)
    mask = member_mask(lengths_ref, offset, seq_count, tok_count)
    place = 0
    for u in range(cfg["hid"]):
        for k in range(cfg["seq"]):
            expert = expert_of(source(column, k, cfg["seq"]), source(core, u, cfg["hid"]), k, cfg)
            parts = [
                jnp.where(mask, mix_ref[pl.ds(expert * per + i, 1), :], 0.0) for i in range(per)
            ]
            wide_ref[pl.ds(place * rows, rows), :] = jnp.concatenate(parts, axis=0)
            place += 1
    table_ref[...] = jnp.transpose(wide_ref[...], (1, 0)).astype(BF16)
    for copy in copies:
        copy.wait()


def mix_kernel(count, table_ref, *refs):
    ins, out, held = refs[:count], refs[count], refs[count + 1]
    rows = ins[0].shape[0]
    done, sems = refs[count + 2 :]
    for k, r in enumerate(ins):
        held[k * rows : (k + 1) * rows, :] = r[...]
    steps = sems.shape[0]
    tile = table_ref.shape[0] // steps
    copies = []
    for i in range(steps):
        part = pl.ds(i * tile, tile)
        done[part, :] = jnp.dot(table_ref[part, :], held[...], preferred_element_type=F32).astype(BF16)
        copy = pltpu.make_async_copy(done.at[part], out.at[0, part], sems.at[i])
        copy.start()
        copies.append(copy)
    for copy in copies:
        copy.wait()


def body(tokens, slot_embed, seq_lengths, w_in, w_out):
    _, tok_count, width = tokens.shape
    slot_count = slot_embed.shape[1]
    seq_count = seq_lengths.shape[1]
    groups, columns, cores = (lax.axis_size(a) for a in ("group", "seq", "hid"))
    per = slot_count // (columns * cores)
    rows = per * seq_count
    all_rows = slot_count * seq_count
    cfg = dict(hid=cores, seq=columns, seqs=seq_count, per=per, chunks=2)

    outs = pl.pallas_call(
        functools.partial(local_kernel, cfg),
        out_shape=[jax.ShapeDtypeStruct((columns * rows, width + STAT), BF16)] * cores
        + [jax.ShapeDtypeStruct((slot_count, tok_count), F32)],
        in_specs=[HBM, HBM, HBM],
        out_specs=[VMEM] * (cores + 1),
        scratch_shapes=[
            pltpu.VMEM((tok_count, width), BF16),
            pltpu.VMEM((slot_count, width), BF16),
            pltpu.SMEM((1, seq_count), jnp.int32),
            pltpu.VMEM((all_rows, tok_count), BF16),
            pltpu.VMEM((all_rows, 1), F32),
            pltpu.VMEM((all_rows, 1), F32),
            pltpu.SemaphoreType.DMA((cfg["chunks"],)),
            pltpu.SemaphoreType.DMA((2,)),
        ],
        compiler_params=params((tok_count * width, 2), (all_rows * tok_count, 4), (all_rows * width, 6)),
        name="local",
    )(far(seq_lengths), far(slot_embed.T), far(tokens))
    sums, logits = outs[:cores], outs[cores]

    table, near_in, near_out = pl.pallas_call(
        functools.partial(table_kernel, cfg),
        out_shape=[
            jax.ShapeDtypeStruct((tok_count, all_rows), BF16),
            jax.ShapeDtypeStruct(w_in.shape, BF16),
            jax.ShapeDtypeStruct(w_out.shape, BF16),
        ],
        in_specs=[SMEM, VMEM, HBM, HBM],
        out_specs=[VMEM] * 3,
        scratch_shapes=[
            pltpu.VMEM((slot_count, tok_count), F32),
            pltpu.VMEM((all_rows, tok_count), F32),
            pltpu.SemaphoreType.DMA((2,)),
        ],
        cost_estimate=pl.CostEstimate(
            flops=8 * all_rows * tok_count, bytes_accessed=4 * all_rows * tok_count, transcendentals=slot_count * tok_count
        ),
        compiler_params=params((all_rows * tok_count, 8), (w_in.size, 4)),
        name="table",
    )(seq_lengths, logits, far(w_in), far(w_out))

    chip = [sums[0]] + [swap(sums[u], "hid", u) for u in range(1, cores)]
    blocks = pl.pallas_call(
        functools.partial(chip_kernel, cores),
        out_shape=[jax.ShapeDtypeStruct((rows, width + STAT), BF16)] * columns,
        in_specs=[VMEM] * cores,
        out_specs=[VMEM] * columns,
        compiler_params=params((all_rows * width, 6)),
        name="chip",
    )(*chip)

    got = [blocks[0]] + [cross(b, "seq", k) for k, b in zip(far_first(columns), blocks) if k]
    own = pl.pallas_call(
        column_kernel,
        out_shape=jax.ShapeDtypeStruct((rows, width), BF16),
        in_specs=[VMEM] * (columns + 1),
        out_specs=VMEM,
        compiler_params=params((all_rows * width, 6)),
        name="column",
    )(*got, table)

    spread = [reflect(own)] + [cross(own, "group", k) for k in range(1, groups)]
    parts = pl.pallas_call(
        functools.partial(expert_kernel, groups),
        out_shape=[jax.ShapeDtypeStruct((rows, width), BF16)] * groups,
        in_specs=[VMEM] * (groups + 2),
        out_specs=[VMEM] * groups,
        compiler_params=params((w_in.size, 2), (w_out.size, 2), (groups * rows * width, 6)),
        name="expert",
    )(*spread, near_in, near_out)
    back = [reflect(parts[0])] + [
        cross(part, "group", k if groups & (groups - 1) == 0 else groups - k)
        for k, part in zip(far_first(groups), parts)
        if k
    ]
    slot_rows = sum(b.astype(F32) for b in back).astype(BF16)

    column_rows = [slot_rows] + [cross(slot_rows, "seq", k) for k in range(1, columns)]
    every = list(column_rows)
    for u in range(1, cores):
        every += [swap(r, "hid", u) for r in column_rows]

    return pl.pallas_call(
        functools.partial(mix_kernel, len(every)),
        out_shape=jax.ShapeDtypeStruct((1, tok_count, width), BF16),
        in_specs=[VMEM] * (1 + len(every)),
        out_specs=HBM,
        scratch_shapes=[
            pltpu.VMEM((all_rows, width), BF16),
            pltpu.VMEM((tok_count, width), BF16),
            pltpu.SemaphoreType.DMA((8,)),
        ],
        compiler_params=params((all_rows * width, 4), (tok_count * width, 4)),
        name="mix",
    )(table, *every)


def solution(mesh):
    placed = (
        P("group", ("seq", "hid"), None),
        P(),
        P("group", None),
        P(("seq", "hid"), None, "group"),
        P(("seq", "hid"), "group", None),
    )
    return jax.shard_map(
        body,
        mesh=mesh,
        in_specs=placed,
        out_specs=P("group", ("seq", "hid"), None),
        check_vma=False,
    )
```

```python
import functools

import jax
import jax.numpy as jnp
from jax import lax
from jax.experimental import pallas as pl
from jax.experimental.pallas import tpu as pltpu
from jax.sharding import PartitionSpec as P


CHIP_VMEM = 67043328
EMPTY = -1e30
STAT = 128
BF16 = jnp.bfloat16
F32 = jnp.float32
VMEM = pl.BlockSpec(memory_space=pltpu.VMEM)
SMEM = pl.BlockSpec(memory_space=pltpu.SMEM)
HBM = pl.BlockSpec(memory_space=pltpu.HBM)


def params(*arrays):
    size = sum(2 * count * each for count, each in arrays)
    return pltpu.CompilerParams(vmem_limit_bytes=int(size) + (4 << 20))


def partner(index, step, size):
    if size & (size - 1) == 0:
        return index ^ step
    return (index + step) % size


def far_first(size):
    return [0] + list(range(size - 1, 0, -1))


def source(index, step, size):
    if size & (size - 1) == 0:
        return index ^ step
    return (index - step) % size


def cuts(count, shares):
    out, begin = [], 0
    for share in shares:
        size = count * share // sum(shares)
        out.append((begin, size))
        begin += size
    return out


def far(value):
    return pltpu.with_memory_space_constraint(value, pltpu.HBM)


def swap(value, axis, step):
    size = lax.axis_size(axis)
    return lax.ppermute(value, axis, [(i, partner(i, step, size)) for i in range(size)])


def mirror(core, cores):
    return cores - 1 - core


def cross(value, axis, step):
    size, cores = lax.axis_size(axis), lax.axis_size("hid")
    pairs = [
        (i * cores + c, partner(i, step, size) * cores + mirror(c, cores))
        for i in range(size)
        for c in range(cores)
    ]
    return lax.ppermute(value, (axis, "hid"), pairs)


def reflect(value):
    cores = lax.axis_size("hid")
    return lax.ppermute(value, "hid", [(c, mirror(c, cores)) for c in range(cores)])


def expert_of(column, core, step, cfg):
    return column * cfg["hid"] + (core if step else mirror(core, cfg["hid"]))


def split3(value):
    high = value.astype(BF16)
    rest = value - high.astype(F32)
    mid = rest.astype(BF16)
    low = (rest - mid.astype(F32)).astype(BF16)
    return high.astype(F32), mid.astype(F32), low.astype(F32)


def pack_stats(peak, total):
    rows = peak.shape[0]
    lane = lax.broadcasted_iota(jnp.int32, (rows, STAT), 1)
    out = jnp.zeros((rows, STAT), F32)
    for at, part in enumerate(split3(peak) + split3(total)):
        out = jnp.where(lane == at, part, out)
    return out.astype(BF16)


def read_stats(block):
    stats = block.astype(F32)
    lane = lax.broadcasted_iota(jnp.int32, stats.shape, 1)
    peak = jnp.sum(jnp.where(lane < 3, stats, 0.0), axis=1, keepdims=True)
    total = jnp.sum(jnp.where((lane >= 3) & (lane < 6), stats, 0.0), axis=1, keepdims=True)
    return peak, total


def member_mask(lengths_ref, offset, seq_count, tok_count):
    row = lax.broadcasted_iota(jnp.int32, (seq_count, tok_count), 0)
    place = offset + lax.broadcasted_iota(jnp.int32, (seq_count, tok_count), 1)
    begin = jnp.int32(0)
    starts = jnp.zeros((seq_count, tok_count), jnp.int32)
    ends = jnp.zeros((seq_count, tok_count), jnp.int32)
    for s in range(seq_count):
        end = begin + lengths_ref[0, s]
        starts = jnp.where(row == s, begin, starts)
        ends = jnp.where(row == s, end, ends)
        begin = end
    return (place >= starts) & (place < ends)


def place_of(cfg, tok_count):
    column, core = lax.axis_index("seq"), lax.axis_index("hid")
    return column, core, (column * cfg["hid"] + core) * tok_count


def local_kernel(cfg, lengths_hbm, embed_hbm, tok_hbm, *refs):
    outs, logits_ref = refs[: cfg["hid"]], refs[cfg["hid"]]
    (tok_ref, embed_ref, lengths_ref, weight_ref, peak_ref, total_ref, sems, small) = refs[
        cfg["hid"] + 1 :
    ]
    tok_count, width = tok_ref.shape
    seq_count, per = cfg["seqs"], cfg["per"]
    rows = per * seq_count
    get_embed = pltpu.make_async_copy(embed_hbm, embed_ref, small.at[0])
    get_embed.start()
    get_lengths = pltpu.make_async_copy(lengths_hbm, lengths_ref, small.at[1])
    get_lengths.start()
    copies = []
    pieces = cuts(width, cfg["chunks"])
    for i, (begin, size) in enumerate(pieces):
        part = pl.ds(begin, size)
        copy = pltpu.make_async_copy(tok_hbm.at[0, :, part], tok_ref.at[:, part], sems.at[i])
        copy.start()
        copies.append(copy)
    column, core, offset = place_of(cfg, tok_count)
    get_lengths.wait()
    mask = member_mask(lengths_ref, offset, seq_count, tok_count)
    get_embed.wait()
    for i, (begin, size) in enumerate(pieces):
        copies[i].wait()
        part = pl.ds(begin, size)
        more = lax.dot_general(
            embed_ref[:, part],
            tok_ref[:, part],
            (((1,), (1,)), ((), ())),
            preferred_element_type=F32,
        )
        logits_ref[...] = more if i == 0 else logits_ref[...] + more
    place = 0
    for u in range(cfg["hid"]):
        for k in range(cfg["seq"]):
            expert = expert_of(partner(column, k, cfg["seq"]), partner(core, u, cfg["hid"]), k, cfg)
            parts, peaks, totals = [], [], []
            for i in range(per):
                row = logits_ref[pl.ds(expert * per + i, 1), :]
                masked = jnp.where(mask, row, EMPTY)
                peak = jnp.max(masked, axis=1, keepdims=True)
                exponent = jnp.where(mask, jnp.exp(masked - peak), 0.0)
                parts.append(exponent)
                peaks.append(peak)
                totals.append(jnp.sum(exponent, axis=1, keepdims=True))
            here = pl.ds(place * rows, rows)
            weight_ref[here, :] = jnp.concatenate(parts, axis=0).astype(BF16)
            peak_ref[here, :] = jnp.concatenate(peaks, axis=0)
            total_ref[here, :] = jnp.concatenate(totals, axis=0)
            place += 1
    each = cfg["seq"] * rows
    full = jnp.dot(weight_ref[...], tok_ref[...], preferred_element_type=F32)
    for u in range(cfg["hid"]):
        here = pl.ds(u * each, each)
        sums = full[u * each : (u + 1) * each]
        total = total_ref[here, :]
        outs[u][:, :width] = (sums * (1.0 / jnp.maximum(total, 1.0))).astype(BF16)
        outs[u][:, width:] = pack_stats(peak_ref[here, :], total)


def merge_blocks(blocks, width):
    stats = [read_stats(b[:, width:]) for b in blocks]
    peak = functools.reduce(jnp.maximum, [s[0] for s in stats])
    weights = [s[1] * jnp.exp(s[0] - peak) for s in stats]
    total = sum(weights)
    inverse = 1.0 / jnp.maximum(total, 1.0)
    merged = sum(b[:, :width].astype(F32) * (w * inverse) for b, w in zip(blocks, weights))
    return merged.astype(BF16), peak, total


def chip_kernel(count, *refs):
    ins, outs = refs[:count], refs[count:]
    rows, wide = outs[0].shape
    width = wide - STAT
    for k, out in zip(far_first(len(outs)), outs):
        here = slice(k * rows, (k + 1) * rows)
        merged, peak, total = merge_blocks([r[here, :] for r in ins], width)
        out[:, :width] = merged
        out[:, width:] = pack_stats(peak, total)


def column_kernel(*refs):
    ins, out = refs[:-2], refs[-1]
    merged, _, _ = merge_blocks([r[...] for r in ins], out.shape[1])
    out[...] = merged


def expert_kernel(count, *refs):
    ins, (w_in_ref, w_out_ref), outs = refs[:count], refs[count : count + 2], refs[count + 2 :]
    rows = ins[0].shape[0]
    picked = jnp.concatenate([r[...] for r in ins], axis=0)
    hidden = jax.nn.gelu(
        jnp.dot(picked, w_in_ref[0], preferred_element_type=F32), approximate=True
    ).astype(BF16)
    result = jnp.dot(hidden, w_out_ref[0], preferred_element_type=F32).astype(BF16)
    for k, out in zip(far_first(len(outs)), outs):
        out[...] = result[k * rows : (k + 1) * rows, :]


def table_kernel(cfg, lengths_ref, logits_ref, *refs):
    loads, (table_ref, *kept), (mix_ref, wide_ref, sems) = refs[:2], refs[2:5], refs[5:]
    copies = [pltpu.make_async_copy(a, b, sems.at[i]) for i, (a, b) in enumerate(zip(loads, kept))]
    for copy in copies:
        copy.start()
    slot_count, tok_count = logits_ref.shape
    seq_count, per = cfg["seqs"], cfg["per"]
    rows = per * seq_count
    logits = logits_ref[...]
    raised = jnp.exp(logits - jnp.max(logits, axis=0, keepdims=True))
    mix_ref[...] = raised / jnp.sum(raised, axis=0, keepdims=True)
    column, core, offset = place_of(cfg, tok_count)
    mask = member_mask(lengths_ref, offset, seq_count, tok_count)
    place = 0
    for u in range(cfg["hid"]):
        for k in range(cfg["seq"]):
            expert = expert_of(source(column, k, cfg["seq"]), source(core, u, cfg["hid"]), k, cfg)
            parts = [
                jnp.where(mask, mix_ref[pl.ds(expert * per + i, 1), :], 0.0) for i in range(per)
            ]
            wide_ref[pl.ds(place * rows, rows), :] = jnp.concatenate(parts, axis=0)
            place += 1
    table_ref[...] = jnp.transpose(wide_ref[...], (1, 0)).astype(BF16)
    for copy in copies:
        copy.wait()


def mix_kernel(count, table_ref, *refs):
    ins, out, held = refs[:count], refs[count], refs[count + 1]
    rows = ins[0].shape[0]
    done, sems = refs[count + 2 :]
    for k, r in enumerate(ins):
        held[k * rows : (k + 1) * rows, :] = r[...]
    steps = sems.shape[0]
    tile = table_ref.shape[0] // steps
    copies = []
    for i in range(steps):
        part = pl.ds(i * tile, tile)
        done[part, :] = jnp.dot(table_ref[part, :], held[...], preferred_element_type=F32).astype(BF16)
        copy = pltpu.make_async_copy(done.at[part], out.at[0, part], sems.at[i])
        copy.start()
        copies.append(copy)
    for copy in copies:
        copy.wait()


def body(tokens, slot_embed, seq_lengths, w_in, w_out):
    _, tok_count, width = tokens.shape
    slot_count = slot_embed.shape[1]
    seq_count = seq_lengths.shape[1]
    groups, columns, cores = (lax.axis_size(a) for a in ("group", "seq", "hid"))
    per = slot_count // (columns * cores)
    rows = per * seq_count
    all_rows = slot_count * seq_count
    cfg = dict(hid=cores, seq=columns, seqs=seq_count, per=per, chunks=(4, 4, 2))

    outs = pl.pallas_call(
        functools.partial(local_kernel, cfg),
        out_shape=[jax.ShapeDtypeStruct((columns * rows, width + STAT), BF16)] * cores
        + [jax.ShapeDtypeStruct((slot_count, tok_count), F32)],
        in_specs=[HBM, HBM, HBM],
        out_specs=[VMEM] * (cores + 1),
        scratch_shapes=[
            pltpu.VMEM((tok_count, width), BF16),
            pltpu.VMEM((slot_count, width), BF16),
            pltpu.SMEM((1, seq_count), jnp.int32),
            pltpu.VMEM((all_rows, tok_count), BF16),
            pltpu.VMEM((all_rows, 1), F32),
            pltpu.VMEM((all_rows, 1), F32),
            pltpu.SemaphoreType.DMA((len(cfg["chunks"]),)),
            pltpu.SemaphoreType.DMA((2,)),
        ],
        compiler_params=params((tok_count * width, 2), (all_rows * tok_count, 4), (all_rows * width, 6)),
        name="local",
    )(far(seq_lengths), far(slot_embed.T), far(tokens))
    sums, logits = outs[:cores], outs[cores]

    table, near_in, near_out = pl.pallas_call(
        functools.partial(table_kernel, cfg),
        out_shape=[
            jax.ShapeDtypeStruct((tok_count, all_rows), BF16),
            jax.ShapeDtypeStruct(w_in.shape, BF16),
            jax.ShapeDtypeStruct(w_out.shape, BF16),
        ],
        in_specs=[SMEM, VMEM, HBM, HBM],
        out_specs=[VMEM] * 3,
        scratch_shapes=[
            pltpu.VMEM((slot_count, tok_count), F32),
            pltpu.VMEM((all_rows, tok_count), F32),
            pltpu.SemaphoreType.DMA((2,)),
        ],
        cost_estimate=pl.CostEstimate(
            flops=8 * all_rows * tok_count, bytes_accessed=4 * all_rows * tok_count, transcendentals=slot_count * tok_count
        ),
        compiler_params=params((all_rows * tok_count, 8), (w_in.size, 4)),
        name="table",
    )(seq_lengths, logits, far(w_in), far(w_out))

    chip = [sums[0]] + [swap(sums[u], "hid", u) for u in range(1, cores)]
    blocks = pl.pallas_call(
        functools.partial(chip_kernel, cores),
        out_shape=[jax.ShapeDtypeStruct((rows, width + STAT), BF16)] * columns,
        in_specs=[VMEM] * cores,
        out_specs=[VMEM] * columns,
        compiler_params=params((all_rows * width, 6)),
        name="chip",
    )(*chip)

    got = [blocks[0]] + [cross(b, "seq", k) for k, b in zip(far_first(columns), blocks) if k]
    own = pl.pallas_call(
        column_kernel,
        out_shape=jax.ShapeDtypeStruct((rows, width), BF16),
        in_specs=[VMEM] * (columns + 1),
        out_specs=VMEM,
        compiler_params=params((all_rows * width, 6)),
        name="column",
    )(*got, table)

    spread = [reflect(own)] + [cross(own, "group", k) for k in range(1, groups)]
    parts = pl.pallas_call(
        functools.partial(expert_kernel, groups),
        out_shape=[jax.ShapeDtypeStruct((rows, width), BF16)] * groups,
        in_specs=[VMEM] * (groups + 2),
        out_specs=[VMEM] * groups,
        compiler_params=params((w_in.size, 2), (w_out.size, 2), (groups * rows * width, 6)),
        name="expert",
    )(*spread, near_in, near_out)
    back = [reflect(parts[0])] + [
        cross(part, "group", k if groups & (groups - 1) == 0 else groups - k)
        for k, part in zip(far_first(groups), parts)
        if k
    ]
    slot_rows = sum(b.astype(F32) for b in back).astype(BF16)

    column_rows = [slot_rows] + [cross(slot_rows, "seq", k) for k in range(1, columns)]
    every = list(column_rows)
    for u in range(1, cores):
        every += [swap(r, "hid", u) for r in column_rows]

    return pl.pallas_call(
        functools.partial(mix_kernel, len(every)),
        out_shape=jax.ShapeDtypeStruct((1, tok_count, width), BF16),
        in_specs=[VMEM] * (1 + len(every)),
        out_specs=HBM,
        scratch_shapes=[
            pltpu.VMEM((all_rows, width), BF16),
            pltpu.VMEM((tok_count, width), BF16),
            pltpu.SemaphoreType.DMA((8,)),
        ],
        compiler_params=params((all_rows * width, 4), (tok_count * width, 4)),
        name="mix",
    )(table, *every)


def solution(mesh):
    placed = (
        P("group", ("seq", "hid"), None),
        P(),
        P("group", None),
        P(("seq", "hid"), None, "group"),
        P(("seq", "hid"), "group", None),
    )
    return jax.shard_map(
        body,
        mesh=mesh,
        in_specs=placed,
        out_specs=P("group", ("seq", "hid"), None),
        check_vma=False,
    )
```

```python
import functools

import jax
import jax.numpy as jnp
from jax import lax
from jax.experimental import pallas as pl
from jax.experimental.pallas import tpu as pltpu
from jax.sharding import PartitionSpec as P


CHIP_VMEM = 67043328
EMPTY = -1e30
STAT = 128
BF16 = jnp.bfloat16
F32 = jnp.float32
VMEM = pl.BlockSpec(memory_space=pltpu.VMEM)
SMEM = pl.BlockSpec(memory_space=pltpu.SMEM)
HBM = pl.BlockSpec(memory_space=pltpu.HBM)


def params(*arrays):
    size = sum(2 * count * each for count, each in arrays)
    return pltpu.CompilerParams(vmem_limit_bytes=int(size) + (4 << 20))


def partner(index, step, size):
    if size & (size - 1) == 0:
        return index ^ step
    return (index + step) % size


def far_first(size):
    return [0] + list(range(size - 1, 0, -1))


def evens_first(size):
    return list(range(0, size, 2)) + list(range(1, size, 2))


def source(index, step, size):
    if size & (size - 1) == 0:
        return index ^ step
    return (index - step) % size


def cuts(count, shares):
    out, begin = [], 0
    for share in shares:
        size = count * share // sum(shares)
        out.append((begin, size))
        begin += size
    return out


def far(value):
    return pltpu.with_memory_space_constraint(value, pltpu.HBM)


def swap(value, axis, step):
    size = lax.axis_size(axis)
    return lax.ppermute(value, axis, [(i, partner(i, step, size)) for i in range(size)])


def mirror(core, cores):
    return cores - 1 - core


def cross(value, axis, step):
    size, cores = lax.axis_size(axis), lax.axis_size("hid")
    pairs = [
        (i * cores + c, partner(i, step, size) * cores + mirror(c, cores))
        for i in range(size)
        for c in range(cores)
    ]
    return lax.ppermute(value, (axis, "hid"), pairs)


def reflect(value):
    cores = lax.axis_size("hid")
    return lax.ppermute(value, "hid", [(c, mirror(c, cores)) for c in range(cores)])


def expert_of(column, core, step, cfg):
    return column * cfg["hid"] + (core if step else mirror(core, cfg["hid"]))


def split3(value):
    high = value.astype(BF16)
    rest = value - high.astype(F32)
    mid = rest.astype(BF16)
    low = (rest - mid.astype(F32)).astype(BF16)
    return high.astype(F32), mid.astype(F32), low.astype(F32)


def pack_stats(peak, total):
    rows = peak.shape[0]
    lane = lax.broadcasted_iota(jnp.int32, (rows, STAT), 1)
    out = jnp.zeros((rows, STAT), F32)
    for at, part in enumerate(split3(peak) + split3(total)):
        out = jnp.where(lane == at, part, out)
    return out.astype(BF16)


def read_stats(block):
    stats = block.astype(F32)
    lane = lax.broadcasted_iota(jnp.int32, stats.shape, 1)
    peak = jnp.sum(jnp.where(lane < 3, stats, 0.0), axis=1, keepdims=True)
    total = jnp.sum(jnp.where((lane >= 3) & (lane < 6), stats, 0.0), axis=1, keepdims=True)
    return peak, total


def member_mask(lengths_ref, offset, seq_count, tok_count):
    row = lax.broadcasted_iota(jnp.int32, (seq_count, tok_count), 0)
    place = offset + lax.broadcasted_iota(jnp.int32, (seq_count, tok_count), 1)
    begin = jnp.int32(0)
    starts = jnp.zeros((seq_count, tok_count), jnp.int32)
    ends = jnp.zeros((seq_count, tok_count), jnp.int32)
    for s in range(seq_count):
        end = begin + lengths_ref[0, s]
        starts = jnp.where(row == s, begin, starts)
        ends = jnp.where(row == s, end, ends)
        begin = end
    return (place >= starts) & (place < ends)


def place_of(cfg, tok_count):
    column, core = lax.axis_index("seq"), lax.axis_index("hid")
    return column, core, (column * cfg["hid"] + core) * tok_count


def local_kernel(cfg, lengths_hbm, embed_hbm, tok_hbm, *refs):
    outs, logits_ref = refs[: cfg["hid"]], refs[cfg["hid"]]
    (tok_ref, embed_ref, lengths_ref, weight_ref, peak_ref, total_ref, sems, small) = refs[
        cfg["hid"] + 1 :
    ]
    tok_count, width = tok_ref.shape
    seq_count, per = cfg["seqs"], cfg["per"]
    rows = per * seq_count
    get_embed = pltpu.make_async_copy(embed_hbm, embed_ref, small.at[0])
    get_embed.start()
    get_lengths = pltpu.make_async_copy(lengths_hbm, lengths_ref, small.at[1])
    get_lengths.start()
    copies = []
    pieces = cuts(width, cfg["chunks"])
    for i, (begin, size) in enumerate(pieces):
        part = pl.ds(begin, size)
        copy = pltpu.make_async_copy(tok_hbm.at[0, :, part], tok_ref.at[:, part], sems.at[i])
        copy.start()
        copies.append(copy)
    column, core, offset = place_of(cfg, tok_count)
    get_lengths.wait()
    mask = member_mask(lengths_ref, offset, seq_count, tok_count)
    get_embed.wait()
    for i, (begin, size) in enumerate(pieces):
        copies[i].wait()
        part = pl.ds(begin, size)
        more = lax.dot_general(
            embed_ref[:, part],
            tok_ref[:, part],
            (((1,), (1,)), ((), ())),
            preferred_element_type=F32,
        )
        logits_ref[...] = more if i == 0 else logits_ref[...] + more
    place = 0
    for u in range(cfg["hid"]):
        for k in range(cfg["seq"]):
            expert = expert_of(partner(column, k, cfg["seq"]), partner(core, u, cfg["hid"]), k, cfg)
            parts, peaks, totals = [], [], []
            for i in range(per):
                row = logits_ref[pl.ds(expert * per + i, 1), :]
                masked = jnp.where(mask, row, EMPTY)
                peak = jnp.max(masked, axis=1, keepdims=True)
                exponent = jnp.where(mask, jnp.exp(masked - peak), 0.0)
                parts.append(exponent)
                peaks.append(peak)
                totals.append(jnp.sum(exponent, axis=1, keepdims=True))
            here = pl.ds(place * rows, rows)
            weight_ref[here, :] = jnp.concatenate(parts, axis=0).astype(BF16)
            peak_ref[here, :] = jnp.concatenate(peaks, axis=0)
            total_ref[here, :] = jnp.concatenate(totals, axis=0)
            place += 1
    each = cfg["seq"] * rows
    full = jnp.dot(weight_ref[...], tok_ref[...], preferred_element_type=F32)
    for u in range(cfg["hid"]):
        here = pl.ds(u * each, each)
        sums = full[u * each : (u + 1) * each]
        total = total_ref[here, :]
        outs[u][:, :width] = (sums * (1.0 / jnp.maximum(total, 1.0))).astype(BF16)
        outs[u][:, width:] = pack_stats(peak_ref[here, :], total)


def merge_blocks(blocks, width):
    stats = [read_stats(b[:, width:]) for b in blocks]
    peak = functools.reduce(jnp.maximum, [s[0] for s in stats])
    weights = [s[1] * jnp.exp(s[0] - peak) for s in stats]
    total = sum(weights)
    inverse = 1.0 / jnp.maximum(total, 1.0)
    merged = sum(b[:, :width].astype(F32) * (w * inverse) for b, w in zip(blocks, weights))
    return merged.astype(BF16), peak, total


def chip_kernel(count, *refs):
    ins, outs = refs[:count], refs[count:]
    rows, wide = outs[0].shape
    width = wide - STAT
    for k, out in zip(far_first(len(outs)), outs):
        here = slice(k * rows, (k + 1) * rows)
        merged, peak, total = merge_blocks([r[here, :] for r in ins], width)
        out[:, :width] = merged
        out[:, width:] = pack_stats(peak, total)


def column_kernel(*refs):
    ins, out = refs[:-2], refs[-1]
    merged, _, _ = merge_blocks([r[...] for r in ins], out.shape[1])
    out[...] = merged


def expert_kernel(count, *refs):
    ins, (w_in_ref, w_out_ref), outs = refs[:count], refs[count : count + 2], refs[count + 2 :]
    rows = ins[0].shape[0]
    picked = jnp.concatenate([r[...] for r in ins], axis=0)
    hidden = jax.nn.gelu(
        jnp.dot(picked, w_in_ref[0], preferred_element_type=F32), approximate=True
    ).astype(BF16)
    result = jnp.dot(hidden, w_out_ref[0], preferred_element_type=F32).astype(BF16)
    for k, out in zip(far_first(len(outs)), outs):
        out[...] = result[k * rows : (k + 1) * rows, :]


def table_kernel(cfg, lengths_ref, logits_ref, *refs):
    loads, (table_ref, *kept), (mix_ref, wide_ref, sems) = refs[:2], refs[2:5], refs[5:]
    copies = [pltpu.make_async_copy(a, b, sems.at[i]) for i, (a, b) in enumerate(zip(loads, kept))]
    for copy in copies:
        copy.start()
    slot_count, tok_count = logits_ref.shape
    seq_count, per = cfg["seqs"], cfg["per"]
    rows = per * seq_count
    logits = logits_ref[...]
    raised = jnp.exp(logits - jnp.max(logits, axis=0, keepdims=True))
    mix_ref[...] = raised / jnp.sum(raised, axis=0, keepdims=True)
    column, core, offset = place_of(cfg, tok_count)
    mask = member_mask(lengths_ref, offset, seq_count, tok_count)
    place = 0
    for u in range(cfg["hid"]):
        for k in range(cfg["seq"]):
            expert = expert_of(source(column, k, cfg["seq"]), source(core, u, cfg["hid"]), k, cfg)
            parts = [
                jnp.where(mask, mix_ref[pl.ds(expert * per + i, 1), :], 0.0) for i in range(per)
            ]
            wide_ref[pl.ds(place * rows, rows), :] = jnp.concatenate(parts, axis=0)
            place += 1
    table_ref[...] = jnp.transpose(wide_ref[...], (1, 0)).astype(BF16)
    for copy in copies:
        copy.wait()


def mix_kernel(count, places, table_ref, *refs):
    ins, out, held = refs[:count], refs[count], refs[count + 1]
    rows = ins[0].shape[0]
    done, sems = refs[count + 2 :]
    for k, r in zip(places, ins):
        held[k * rows : (k + 1) * rows, :] = r[...]
    steps = sems.shape[0]
    tile = table_ref.shape[0] // steps
    copies = []
    for i in range(steps):
        part = pl.ds(i * tile, tile)
        done[part, :] = jnp.dot(table_ref[part, :], held[...], preferred_element_type=F32).astype(BF16)
        copy = pltpu.make_async_copy(done.at[part], out.at[0, part], sems.at[i])
        copy.start()
        copies.append(copy)
    for copy in copies:
        copy.wait()


def body(tokens, slot_embed, seq_lengths, w_in, w_out):
    _, tok_count, width = tokens.shape
    slot_count = slot_embed.shape[1]
    seq_count = seq_lengths.shape[1]
    groups, columns, cores = (lax.axis_size(a) for a in ("group", "seq", "hid"))
    per = slot_count // (columns * cores)
    rows = per * seq_count
    all_rows = slot_count * seq_count
    cfg = dict(hid=cores, seq=columns, seqs=seq_count, per=per, chunks=(4, 4, 2))

    outs = pl.pallas_call(
        functools.partial(local_kernel, cfg),
        out_shape=[jax.ShapeDtypeStruct((columns * rows, width + STAT), BF16)] * cores
        + [jax.ShapeDtypeStruct((slot_count, tok_count), F32)],
        in_specs=[HBM, HBM, HBM],
        out_specs=[VMEM] * (cores + 1),
        scratch_shapes=[
            pltpu.VMEM((tok_count, width), BF16),
            pltpu.VMEM((slot_count, width), BF16),
            pltpu.SMEM((1, seq_count), jnp.int32),
            pltpu.VMEM((all_rows, tok_count), BF16),
            pltpu.VMEM((all_rows, 1), F32),
            pltpu.VMEM((all_rows, 1), F32),
            pltpu.SemaphoreType.DMA((len(cfg["chunks"]),)),
            pltpu.SemaphoreType.DMA((2,)),
        ],
        compiler_params=params((tok_count * width, 2), (all_rows * tok_count, 4), (all_rows * width, 6)),
        name="local",
    )(far(seq_lengths), far(slot_embed.T), far(tokens))
    sums, logits = outs[:cores], outs[cores]

    table, near_in, near_out = pl.pallas_call(
        functools.partial(table_kernel, cfg),
        out_shape=[
            jax.ShapeDtypeStruct((tok_count, all_rows), BF16),
            jax.ShapeDtypeStruct(w_in.shape, BF16),
            jax.ShapeDtypeStruct(w_out.shape, BF16),
        ],
        in_specs=[SMEM, VMEM, HBM, HBM],
        out_specs=[VMEM] * 3,
        scratch_shapes=[
            pltpu.VMEM((slot_count, tok_count), F32),
            pltpu.VMEM((all_rows, tok_count), F32),
            pltpu.SemaphoreType.DMA((2,)),
        ],
        cost_estimate=pl.CostEstimate(
            flops=8 * all_rows * tok_count, bytes_accessed=4 * all_rows * tok_count, transcendentals=slot_count * tok_count
        ),
        compiler_params=params((all_rows * tok_count, 8), (w_in.size, 4)),
        name="table",
    )(seq_lengths, logits, far(w_in), far(w_out))

    chip = [sums[0]] + [swap(sums[u], "hid", u) for u in range(1, cores)]
    blocks = pl.pallas_call(
        functools.partial(chip_kernel, cores),
        out_shape=[jax.ShapeDtypeStruct((rows, width + STAT), BF16)] * columns,
        in_specs=[VMEM] * cores,
        out_specs=[VMEM] * columns,
        compiler_params=params((all_rows * width, 6)),
        name="chip",
    )(*chip)

    got = [blocks[0]] + [cross(b, "seq", k) for k, b in zip(far_first(columns), blocks) if k]
    own = pl.pallas_call(
        column_kernel,
        out_shape=jax.ShapeDtypeStruct((rows, width), BF16),
        in_specs=[VMEM] * (columns + 1),
        out_specs=VMEM,
        compiler_params=params((all_rows * width, 6)),
        name="column",
    )(*got, table)

    spread = [reflect(own)] + [cross(own, "group", k) for k in range(1, groups)]
    parts = pl.pallas_call(
        functools.partial(expert_kernel, groups),
        out_shape=[jax.ShapeDtypeStruct((rows, width), BF16)] * groups,
        in_specs=[VMEM] * (groups + 2),
        out_specs=[VMEM] * groups,
        compiler_params=params((w_in.size, 2), (w_out.size, 2), (groups * rows * width, 6)),
        name="expert",
    )(*spread, near_in, near_out)
    back = [reflect(parts[0])] + [
        cross(part, "group", k if groups & (groups - 1) == 0 else groups - k)
        for k, part in zip(far_first(groups), parts)
        if k
    ]
    slot_rows = sum(b.astype(F32) for b in back).astype(BF16)

    column_rows = [slot_rows] + [cross(slot_rows, "seq", k) for k in range(1, columns)]
    every = list(column_rows)
    places = [u * columns + k for u in range(cores) for k in evens_first(columns)]
    for u in range(1, cores):
        every += [swap(r, "hid", u) for r in column_rows]

    return pl.pallas_call(
        functools.partial(mix_kernel, len(every), places),
        out_shape=jax.ShapeDtypeStruct((1, tok_count, width), BF16),
        in_specs=[VMEM] * (1 + len(every)),
        out_specs=HBM,
        scratch_shapes=[
            pltpu.VMEM((all_rows, width), BF16),
            pltpu.VMEM((tok_count, width), BF16),
            pltpu.SemaphoreType.DMA((8,)),
        ],
        compiler_params=params((all_rows * width, 4), (tok_count * width, 4)),
        name="mix",
    )(table, *[every[k] for k in places])


def solution(mesh):
    placed = (
        P("group", ("seq", "hid"), None),
        P(),
        P("group", None),
        P(("seq", "hid"), None, "group"),
        P(("seq", "hid"), "group", None),
    )
    return jax.shard_map(
        body,
        mesh=mesh,
        in_specs=placed,
        out_specs=P("group", ("seq", "hid"), None),
        check_vma=False,
    )
```

```python
import functools

import jax
import jax.numpy as jnp
from jax import lax
from jax.experimental import pallas as pl
from jax.experimental.pallas import tpu as pltpu
from jax.sharding import PartitionSpec as P


CHIP_VMEM = 67043328
EMPTY = -1e30
STAT = 128
BF16 = jnp.bfloat16
F32 = jnp.float32
VMEM = pl.BlockSpec(memory_space=pltpu.VMEM)
SMEM = pl.BlockSpec(memory_space=pltpu.SMEM)
HBM = pl.BlockSpec(memory_space=pltpu.HBM)


def params(*arrays):
    size = sum(2 * count * each for count, each in arrays)
    return pltpu.CompilerParams(vmem_limit_bytes=int(size) + (4 << 20))


def partner(index, step, size):
    if size & (size - 1) == 0:
        return index ^ step
    return (index + step) % size


def far_first(size):
    return [0] + list(range(size - 1, 0, -1))


def evens_first(size):
    return list(range(0, size, 2)) + list(range(1, size, 2))


def source(index, step, size):
    if size & (size - 1) == 0:
        return index ^ step
    return (index - step) % size


def cuts(count, shares):
    out, begin = [], 0
    for share in shares:
        size = count * share // sum(shares)
        out.append((begin, size))
        begin += size
    return out


def far(value):
    return pltpu.with_memory_space_constraint(value, pltpu.HBM)


def swap(value, axis, step):
    size = lax.axis_size(axis)
    return lax.ppermute(value, axis, [(i, partner(i, step, size)) for i in range(size)])


def mirror(core, cores):
    return cores - 1 - core


def cross(value, axis, step):
    size, cores = lax.axis_size(axis), lax.axis_size("hid")
    pairs = [
        (i * cores + c, partner(i, step, size) * cores + mirror(c, cores))
        for i in range(size)
        for c in range(cores)
    ]
    return lax.ppermute(value, (axis, "hid"), pairs)


def reflect(value):
    cores = lax.axis_size("hid")
    return lax.ppermute(value, "hid", [(c, mirror(c, cores)) for c in range(cores)])


def expert_of(column, core, step, cfg):
    return column * cfg["hid"] + (core if step else mirror(core, cfg["hid"]))


def split3(value):
    high = value.astype(BF16)
    rest = value - high.astype(F32)
    mid = rest.astype(BF16)
    low = (rest - mid.astype(F32)).astype(BF16)
    return high.astype(F32), mid.astype(F32), low.astype(F32)


def pack_stats(peak, total):
    rows = peak.shape[0]
    lane = lax.broadcasted_iota(jnp.int32, (rows, STAT), 1)
    out = jnp.zeros((rows, STAT), F32)
    for at, part in enumerate(split3(peak) + split3(total)):
        out = jnp.where(lane == at, part, out)
    return out.astype(BF16)


def read_stats(block):
    stats = block.astype(F32)
    lane = lax.broadcasted_iota(jnp.int32, stats.shape, 1)
    peak = jnp.sum(jnp.where(lane < 3, stats, 0.0), axis=1, keepdims=True)
    total = jnp.sum(jnp.where((lane >= 3) & (lane < 6), stats, 0.0), axis=1, keepdims=True)
    return peak, total


def member_mask(lengths_ref, offset, seq_count, tok_count):
    row = lax.broadcasted_iota(jnp.int32, (seq_count, tok_count), 0)
    place = offset + lax.broadcasted_iota(jnp.int32, (seq_count, tok_count), 1)
    begin = jnp.int32(0)
    starts = jnp.zeros((seq_count, tok_count), jnp.int32)
    ends = jnp.zeros((seq_count, tok_count), jnp.int32)
    for s in range(seq_count):
        end = begin + lengths_ref[0, s]
        starts = jnp.where(row == s, begin, starts)
        ends = jnp.where(row == s, end, ends)
        begin = end
    return (place >= starts) & (place < ends)


def place_of(cfg, tok_count):
    column, core = lax.axis_index("seq"), lax.axis_index("hid")
    return column, core, (column * cfg["hid"] + core) * tok_count


def local_kernel(cfg, lengths_hbm, embed_hbm, tok_hbm, *refs):
    outs, logits_ref = refs[: cfg["hid"]], refs[cfg["hid"]]
    (tok_ref, embed_ref, lengths_ref, weight_ref, peak_ref, total_ref, sems, small) = refs[
        cfg["hid"] + 1 :
    ]
    tok_count, width = tok_ref.shape
    seq_count, per = cfg["seqs"], cfg["per"]
    rows = per * seq_count
    get_embed = pltpu.make_async_copy(embed_hbm, embed_ref, small.at[0])
    get_embed.start()
    get_lengths = pltpu.make_async_copy(lengths_hbm, lengths_ref, small.at[1])
    get_lengths.start()
    copies = []
    pieces = cuts(width, cfg["chunks"])
    for i, (begin, size) in enumerate(pieces):
        part = pl.ds(begin, size)
        copy = pltpu.make_async_copy(tok_hbm.at[0, :, part], tok_ref.at[:, part], sems.at[i])
        copy.start()
        copies.append(copy)
    column, core, offset = place_of(cfg, tok_count)
    get_lengths.wait()
    mask = member_mask(lengths_ref, offset, seq_count, tok_count)
    get_embed.wait()
    for i, (begin, size) in enumerate(pieces):
        copies[i].wait()
        part = pl.ds(begin, size)
        more = lax.dot_general(
            embed_ref[:, part],
            tok_ref[:, part],
            (((1,), (1,)), ((), ())),
            preferred_element_type=F32,
        )
        logits_ref[...] = more if i == 0 else logits_ref[...] + more
    place = 0
    for u in range(cfg["hid"]):
        for k in range(cfg["seq"]):
            expert = expert_of(partner(column, k, cfg["seq"]), partner(core, u, cfg["hid"]), k, cfg)
            parts, peaks, totals = [], [], []
            for i in range(per):
                row = logits_ref[pl.ds(expert * per + i, 1), :]
                masked = jnp.where(mask, row, EMPTY)
                peak = jnp.max(masked, axis=1, keepdims=True)
                exponent = jnp.where(mask, jnp.exp(masked - peak), 0.0)
                parts.append(exponent)
                peaks.append(peak)
                totals.append(jnp.sum(exponent, axis=1, keepdims=True))
            here = pl.ds(place * rows, rows)
            weight_ref[here, :] = jnp.concatenate(parts, axis=0).astype(BF16)
            peak_ref[here, :] = jnp.concatenate(peaks, axis=0)
            total_ref[here, :] = jnp.concatenate(totals, axis=0)
            place += 1
    each = cfg["seq"] * rows
    full = jnp.dot(weight_ref[...], tok_ref[...], preferred_element_type=F32)
    for u in range(cfg["hid"]):
        here = pl.ds(u * each, each)
        sums = full[u * each : (u + 1) * each]
        total = total_ref[here, :]
        outs[u][:, :width] = (sums * (1.0 / jnp.maximum(total, 1.0))).astype(BF16)
        outs[u][:, width:] = pack_stats(peak_ref[here, :], total)


def merge_blocks(blocks, width):
    stats = [read_stats(b[:, width:]) for b in blocks]
    peak = functools.reduce(jnp.maximum, [s[0] for s in stats])
    weights = [s[1] * jnp.exp(s[0] - peak) for s in stats]
    total = sum(weights)
    inverse = 1.0 / jnp.maximum(total, 1.0)
    merged = sum(b[:, :width].astype(F32) * (w * inverse) for b, w in zip(blocks, weights))
    return merged.astype(BF16), peak, total


def chip_kernel(count, *refs):
    ins, outs = refs[:count], refs[count:]
    rows, wide = outs[0].shape
    width = wide - STAT
    for k, out in zip(far_first(len(outs)), outs):
        here = slice(k * rows, (k + 1) * rows)
        merged, peak, total = merge_blocks([r[here, :] for r in ins], width)
        out[:, :width] = merged
        out[:, width:] = pack_stats(peak, total)


def column_kernel(*refs):
    ins, out = refs[:-2], refs[-1]
    merged, _, _ = merge_blocks([r[...] for r in ins], out.shape[1])
    out[...] = merged


def expert_kernel(count, *refs):
    ins, (w_in_ref, w_out_ref), outs = refs[:count], refs[count : count + 2], refs[count + 3 :]
    rows = ins[0].shape[0]
    picked = jnp.concatenate([r[...] for r in ins], axis=0)
    hidden = jax.nn.gelu(
        jnp.dot(picked, w_in_ref[0], preferred_element_type=F32), approximate=True
    ).astype(BF16)
    result = jnp.dot(hidden, w_out_ref[0], preferred_element_type=F32).astype(BF16)
    for k, out in zip(far_first(len(outs)), outs):
        out[...] = result[k * rows : (k + 1) * rows, :]


def table_kernel(cfg, lengths_ref, logits_ref, *refs):
    _, table_ref, mix_ref, wide_ref = refs
    slot_count, tok_count = logits_ref.shape
    seq_count, per = cfg["seqs"], cfg["per"]
    rows = per * seq_count
    logits = logits_ref[...]
    raised = jnp.exp(logits - jnp.max(logits, axis=0, keepdims=True))
    mix_ref[...] = raised / jnp.sum(raised, axis=0, keepdims=True)
    column, core, offset = place_of(cfg, tok_count)
    mask = member_mask(lengths_ref, offset, seq_count, tok_count)
    place = 0
    for u in range(cfg["hid"]):
        for k in range(cfg["seq"]):
            expert = expert_of(source(column, k, cfg["seq"]), source(core, u, cfg["hid"]), k, cfg)
            parts = [
                jnp.where(mask, mix_ref[pl.ds(expert * per + i, 1), :], 0.0) for i in range(per)
            ]
            wide_ref[pl.ds(place * rows, rows), :] = jnp.concatenate(parts, axis=0)
            place += 1
    table_ref[...] = jnp.transpose(wide_ref[...], (1, 0)).astype(BF16)


def load_kernel(_, far_ref, near_ref, sem):
    copy = pltpu.make_async_copy(far_ref, near_ref, sem)
    copy.start()
    copy.wait()


def bring(after, weights):
    return pl.pallas_call(
        load_kernel,
        out_shape=jax.ShapeDtypeStruct(weights.shape, BF16),
        in_specs=[VMEM, HBM],
        out_specs=VMEM,
        scratch_shapes=[pltpu.SemaphoreType.DMA],
        compiler_params=params((weights.size, 2)),
        cost_estimate=pl.CostEstimate(flops=0, bytes_accessed=4 * weights.size, transcendentals=0),
        name="load",
    )(after, far(weights))


def mix_kernel(count, places, table_ref, *refs):
    ins, out, held = refs[:count], refs[count], refs[count + 1]
    rows = ins[0].shape[0]
    done, sems = refs[count + 2 :]
    for k, r in zip(places, ins):
        held[k * rows : (k + 1) * rows, :] = r[...]
    steps = sems.shape[0]
    tile = table_ref.shape[0] // steps
    copies = []
    for i in range(steps):
        part = pl.ds(i * tile, tile)
        done[part, :] = jnp.dot(table_ref[part, :], held[...], preferred_element_type=F32).astype(BF16)
        copy = pltpu.make_async_copy(done.at[part], out.at[0, part], sems.at[i])
        copy.start()
        copies.append(copy)
    for copy in copies:
        copy.wait()


def body(tokens, slot_embed, seq_lengths, w_in, w_out):
    _, tok_count, width = tokens.shape
    slot_count = slot_embed.shape[1]
    seq_count = seq_lengths.shape[1]
    groups, columns, cores = (lax.axis_size(a) for a in ("group", "seq", "hid"))
    per = slot_count // (columns * cores)
    rows = per * seq_count
    all_rows = slot_count * seq_count
    cfg = dict(hid=cores, seq=columns, seqs=seq_count, per=per, chunks=(4, 4, 2))

    outs = pl.pallas_call(
        functools.partial(local_kernel, cfg),
        out_shape=[jax.ShapeDtypeStruct((columns * rows, width + STAT), BF16)] * cores
        + [jax.ShapeDtypeStruct((slot_count, tok_count), F32)],
        in_specs=[HBM, HBM, HBM],
        out_specs=[VMEM] * (cores + 1),
        scratch_shapes=[
            pltpu.VMEM((tok_count, width), BF16),
            pltpu.VMEM((slot_count, width), BF16),
            pltpu.SMEM((1, seq_count), jnp.int32),
            pltpu.VMEM((all_rows, tok_count), BF16),
            pltpu.VMEM((all_rows, 1), F32),
            pltpu.VMEM((all_rows, 1), F32),
            pltpu.SemaphoreType.DMA((len(cfg["chunks"]),)),
            pltpu.SemaphoreType.DMA((2,)),
        ],
        compiler_params=params((tok_count * width, 2), (all_rows * tok_count, 4), (all_rows * width, 6)),
        name="local",
    )(far(seq_lengths), far(slot_embed.T), far(tokens))
    sums, logits = outs[:cores], outs[cores]

    chip = [sums[0]] + [swap(sums[u], "hid", u) for u in range(1, cores)]
    blocks = pl.pallas_call(
        functools.partial(chip_kernel, cores),
        out_shape=[jax.ShapeDtypeStruct((rows, width + STAT), BF16)] * columns,
        in_specs=[VMEM] * cores,
        out_specs=[VMEM] * columns,
        compiler_params=params((all_rows * width, 6)),
        name="chip",
    )(*chip)

    near_in = bring(blocks[0], w_in)
    got = [blocks[0]] + [cross(b, "seq", k) for k, b in zip(far_first(columns), blocks) if k]
    own = pl.pallas_call(
        column_kernel,
        out_shape=jax.ShapeDtypeStruct((rows, width), BF16),
        in_specs=[VMEM] * (columns + 1),
        out_specs=VMEM,
        compiler_params=params((all_rows * width, 6)),
        name="column",
    )(*got, near_in)

    near_out = bring(own, w_out)
    table = pl.pallas_call(
        functools.partial(table_kernel, cfg),
        out_shape=jax.ShapeDtypeStruct((tok_count, all_rows), BF16),
        in_specs=[SMEM, VMEM, VMEM],
        out_specs=VMEM,
        scratch_shapes=[
            pltpu.VMEM((slot_count, tok_count), F32),
            pltpu.VMEM((all_rows, tok_count), F32),
        ],
        compiler_params=params((all_rows * tok_count, 8)),
        cost_estimate=pl.CostEstimate(
            flops=8 * all_rows * tok_count,
            bytes_accessed=4 * all_rows * tok_count,
            transcendentals=slot_count * tok_count,
        ),
        name="table",
    )(seq_lengths, logits, own)

    spread = [reflect(own)] + [cross(own, "group", k) for k in range(1, groups)]
    parts = pl.pallas_call(
        functools.partial(expert_kernel, groups),
        out_shape=[jax.ShapeDtypeStruct((rows, width), BF16)] * groups,
        in_specs=[VMEM] * (groups + 3),
        out_specs=[VMEM] * groups,
        compiler_params=params((w_in.size, 2), (w_out.size, 2), (groups * rows * width, 6)),
        name="expert",
    )(*spread, near_in, near_out, table)
    back = [
        cross(part, "group", k if groups & (groups - 1) == 0 else groups - k)
        for k, part in zip(far_first(groups), parts)
        if k
    ] + [reflect(parts[0])]
    slot_rows = sum(b.astype(F32) for b in back).astype(BF16)

    column_rows = [slot_rows] + [cross(slot_rows, "seq", k) for k in range(1, columns)]
    every = list(column_rows)
    places = [u * columns + k for u in range(cores) for k in evens_first(columns)]
    for u in range(1, cores):
        every += [swap(r, "hid", u) for r in column_rows]

    return pl.pallas_call(
        functools.partial(mix_kernel, len(every), places),
        out_shape=jax.ShapeDtypeStruct((1, tok_count, width), BF16),
        in_specs=[VMEM] * (1 + len(every)),
        out_specs=HBM,
        scratch_shapes=[
            pltpu.VMEM((all_rows, width), BF16),
            pltpu.VMEM((tok_count, width), BF16),
            pltpu.SemaphoreType.DMA((8,)),
        ],
        compiler_params=params((all_rows * width, 4), (tok_count * width, 4)),
        name="mix",
    )(table, *[every[k] for k in places])


def solution(mesh):
    placed = (
        P("group", ("seq", "hid"), None),
        P(),
        P("group", None),
        P(("seq", "hid"), None, "group"),
        P(("seq", "hid"), "group", None),
    )
    return jax.shard_map(
        body,
        mesh=mesh,
        in_specs=placed,
        out_specs=P("group", ("seq", "hid"), None),
        check_vma=False,
    )
```

```python
import functools

import jax
import jax.numpy as jnp
from jax import lax
from jax.experimental import pallas as pl
from jax.experimental.pallas import tpu as pltpu
from jax.sharding import PartitionSpec as P


CHIP_VMEM = 67043328
EMPTY = -1e30
STAT = 128
BF16 = jnp.bfloat16
F32 = jnp.float32
VMEM = pl.BlockSpec(memory_space=pltpu.VMEM)
SMEM = pl.BlockSpec(memory_space=pltpu.SMEM)
HBM = pl.BlockSpec(memory_space=pltpu.HBM)


def params(*arrays):
    size = sum(2 * count * each for count, each in arrays)
    return pltpu.CompilerParams(vmem_limit_bytes=int(size) + (4 << 20))


def partner(index, step, size):
    if size & (size - 1) == 0:
        return index ^ step
    return (index + step) % size


def far_first(size):
    return [0] + list(range(size - 1, 0, -1))


def evens_first(size):
    return list(range(0, size, 2)) + list(range(1, size, 2))


def source(index, step, size):
    if size & (size - 1) == 0:
        return index ^ step
    return (index - step) % size


def cuts(count, shares):
    out, begin = [], 0
    for share in shares:
        size = count * share // sum(shares)
        out.append((begin, size))
        begin += size
    return out


def far(value):
    return pltpu.with_memory_space_constraint(value, pltpu.HBM)


def swap(value, axis, step):
    size = lax.axis_size(axis)
    return lax.ppermute(value, axis, [(i, partner(i, step, size)) for i in range(size)])


def mirror(core, cores):
    return cores - 1 - core


def cross(value, axis, step):
    size, cores = lax.axis_size(axis), lax.axis_size("hid")
    pairs = [
        (i * cores + c, partner(i, step, size) * cores + mirror(c, cores))
        for i in range(size)
        for c in range(cores)
    ]
    return lax.ppermute(value, (axis, "hid"), pairs)


def reflect(value):
    cores = lax.axis_size("hid")
    return lax.ppermute(value, "hid", [(c, mirror(c, cores)) for c in range(cores)])


def expert_of(column, core, step, cfg):
    return column * cfg["hid"] + (core if step else mirror(core, cfg["hid"]))


def split3(value):
    high = value.astype(BF16)
    rest = value - high.astype(F32)
    mid = rest.astype(BF16)
    low = (rest - mid.astype(F32)).astype(BF16)
    return high.astype(F32), mid.astype(F32), low.astype(F32)


def pack_stats(peak, total):
    rows = peak.shape[0]
    lane = lax.broadcasted_iota(jnp.int32, (rows, STAT), 1)
    out = jnp.zeros((rows, STAT), F32)
    for at, part in enumerate(split3(peak) + split3(total)):
        out = jnp.where(lane == at, part, out)
    return out.astype(BF16)


def read_stats(block):
    stats = block.astype(F32)
    lane = lax.broadcasted_iota(jnp.int32, stats.shape, 1)
    peak = jnp.sum(jnp.where(lane < 3, stats, 0.0), axis=1, keepdims=True)
    total = jnp.sum(jnp.where((lane >= 3) & (lane < 6), stats, 0.0), axis=1, keepdims=True)
    return peak, total


def member_mask(lengths_ref, offset, seq_count, tok_count):
    row = lax.broadcasted_iota(jnp.int32, (seq_count, tok_count), 0)
    place = offset + lax.broadcasted_iota(jnp.int32, (seq_count, tok_count), 1)
    begin = jnp.int32(0)
    starts = jnp.zeros((seq_count, tok_count), jnp.int32)
    ends = jnp.zeros((seq_count, tok_count), jnp.int32)
    for s in range(seq_count):
        end = begin + lengths_ref[0, s]
        starts = jnp.where(row == s, begin, starts)
        ends = jnp.where(row == s, end, ends)
        begin = end
    return (place >= starts) & (place < ends)


def place_of(cfg, tok_count):
    column, core = lax.axis_index("seq"), lax.axis_index("hid")
    return column, core, (column * cfg["hid"] + core) * tok_count


def local_kernel(cfg, lengths_hbm, embed_hbm, tok_hbm, *refs):
    outs, logits_ref = refs[: cfg["hid"]], refs[cfg["hid"]]
    (tok_ref, embed_ref, lengths_ref, weight_ref, peak_ref, total_ref, sems, small) = refs[
        cfg["hid"] + 1 :
    ]
    tok_count, width = tok_ref.shape
    seq_count, per = cfg["seqs"], cfg["per"]
    rows = per * seq_count
    get_embed = pltpu.make_async_copy(embed_hbm, embed_ref, small.at[0])
    get_embed.start()
    get_lengths = pltpu.make_async_copy(lengths_hbm, lengths_ref, small.at[1])
    get_lengths.start()
    copies = []
    pieces = cuts(width, cfg["chunks"])
    for i, (begin, size) in enumerate(pieces):
        part = pl.ds(begin, size)
        copy = pltpu.make_async_copy(tok_hbm.at[0, :, part], tok_ref.at[:, part], sems.at[i])
        copy.start()
        copies.append(copy)
    column, core, offset = place_of(cfg, tok_count)
    get_lengths.wait()
    mask = member_mask(lengths_ref, offset, seq_count, tok_count)
    get_embed.wait()
    for i, (begin, size) in enumerate(pieces):
        copies[i].wait()
        part = pl.ds(begin, size)
        more = lax.dot_general(
            embed_ref[:, part],
            tok_ref[:, part],
            (((1,), (1,)), ((), ())),
            preferred_element_type=F32,
        )
        logits_ref[...] = more if i == 0 else logits_ref[...] + more
    place = 0
    for u in range(cfg["hid"]):
        for k in range(cfg["seq"]):
            expert = expert_of(partner(column, k, cfg["seq"]), partner(core, u, cfg["hid"]), k, cfg)
            parts, peaks, totals = [], [], []
            for i in range(per):
                row = logits_ref[pl.ds(expert * per + i, 1), :]
                masked = jnp.where(mask, row, EMPTY)
                peak = jnp.max(masked, axis=1, keepdims=True)
                exponent = jnp.exp(masked - jnp.maximum(peak, EMPTY / 2))
                parts.append(exponent)
                peaks.append(peak)
                totals.append(jnp.sum(exponent, axis=1, keepdims=True))
            here = pl.ds(place * rows, rows)
            weight_ref[here, :] = jnp.concatenate(parts, axis=0).astype(BF16)
            peak_ref[here, :] = jnp.concatenate(peaks, axis=0)
            total_ref[here, :] = jnp.concatenate(totals, axis=0)
            place += 1
    each = cfg["seq"] * rows
    full = jnp.dot(weight_ref[...], tok_ref[...], preferred_element_type=F32)
    for u in range(cfg["hid"]):
        here = pl.ds(u * each, each)
        sums = full[u * each : (u + 1) * each]
        total = total_ref[here, :]
        outs[u][:, :width] = (sums * (1.0 / jnp.maximum(total, 1.0))).astype(BF16)
        outs[u][:, width:] = pack_stats(peak_ref[here, :], total)


def merge_blocks(blocks, width):
    stats = [read_stats(b[:, width:]) for b in blocks]
    peak = functools.reduce(jnp.maximum, [s[0] for s in stats])
    weights = [s[1] * jnp.exp(s[0] - peak) for s in stats]
    total = sum(weights)
    inverse = 1.0 / jnp.maximum(total, 1.0)
    merged = sum(b[:, :width].astype(F32) * (w * inverse) for b, w in zip(blocks, weights))
    return merged.astype(BF16), peak, total


def chip_kernel(count, *refs):
    ins, outs = refs[:count], refs[count:]
    rows, wide = outs[0].shape
    width = wide - STAT
    for k, out in zip(far_first(len(outs)), outs):
        here = slice(k * rows, (k + 1) * rows)
        merged, peak, total = merge_blocks([r[here, :] for r in ins], width)
        out[:, :width] = merged
        out[:, width:] = pack_stats(peak, total)


def column_kernel(*refs):
    ins, out = refs[:-2], refs[-1]
    merged, _, _ = merge_blocks([r[...] for r in ins], out.shape[1])
    out[...] = merged


def expert_kernel(count, *refs):
    ins, (w_in_ref, w_out_ref), outs = refs[:count], refs[count : count + 2], refs[count + 3 :]
    rows = ins[0].shape[0]
    picked = jnp.concatenate([r[...] for r in ins], axis=0)
    hidden = jax.nn.gelu(
        jnp.dot(picked, w_in_ref[0], preferred_element_type=F32), approximate=True
    ).astype(BF16)
    result = jnp.dot(hidden, w_out_ref[0], preferred_element_type=F32).astype(BF16)
    for k, out in zip(far_first(len(outs)), outs):
        out[...] = result[k * rows : (k + 1) * rows, :]


def table_kernel(cfg, lengths_ref, logits_ref, *refs):
    _, table_ref, mix_ref, wide_ref = refs
    slot_count, tok_count = logits_ref.shape
    seq_count, per = cfg["seqs"], cfg["per"]
    rows = per * seq_count
    logits = logits_ref[...]
    raised = jnp.exp(logits - jnp.max(logits, axis=0, keepdims=True))
    mix_ref[...] = raised / jnp.sum(raised, axis=0, keepdims=True)
    column, core, offset = place_of(cfg, tok_count)
    mask = member_mask(lengths_ref, offset, seq_count, tok_count)
    place = 0
    for u in range(cfg["hid"]):
        for k in range(cfg["seq"]):
            expert = expert_of(source(column, k, cfg["seq"]), source(core, u, cfg["hid"]), k, cfg)
            parts = [
                jnp.where(mask, mix_ref[pl.ds(expert * per + i, 1), :], 0.0) for i in range(per)
            ]
            wide_ref[pl.ds(place * rows, rows), :] = jnp.concatenate(parts, axis=0)
            place += 1
    table_ref[...] = jnp.transpose(wide_ref[...], (1, 0)).astype(BF16)


def load_kernel(_, far_ref, near_ref, sem):
    copy = pltpu.make_async_copy(far_ref, near_ref, sem)
    copy.start()
    copy.wait()


def bring(after, weights):
    return pl.pallas_call(
        load_kernel,
        out_shape=jax.ShapeDtypeStruct(weights.shape, BF16),
        in_specs=[VMEM, HBM],
        out_specs=VMEM,
        scratch_shapes=[pltpu.SemaphoreType.DMA],
        compiler_params=params((weights.size, 2)),
        cost_estimate=pl.CostEstimate(flops=0, bytes_accessed=4 * weights.size, transcendentals=0),
        name="load",
    )(after, far(weights))


def mix_kernel(count, places, table_ref, *refs):
    ins, out, held = refs[:count], refs[count], refs[count + 1]
    rows = ins[0].shape[0]
    done, sems = refs[count + 2 :]
    for k, r in zip(places, ins):
        held[k * rows : (k + 1) * rows, :] = r[...]
    steps = sems.shape[0] - 1
    tile = table_ref.shape[0] // steps
    copies = []
    ends = [tile // 2, tile] + [tile * k for k in range(2, steps)] + [tile * steps]
    begin = 0
    for i, end in enumerate(ends):
        part = pl.ds(begin, end - begin)
        begin = end
        done[part, :] = jnp.dot(table_ref[part, :], held[...], preferred_element_type=F32).astype(BF16)
        copy = pltpu.make_async_copy(done.at[part], out.at[0, part], sems.at[i])
        copy.start()
        copies.append(copy)
    for copy in copies:
        copy.wait()


def body(tokens, slot_embed, seq_lengths, w_in, w_out):
    _, tok_count, width = tokens.shape
    slot_count = slot_embed.shape[1]
    seq_count = seq_lengths.shape[1]
    groups, columns, cores = (lax.axis_size(a) for a in ("group", "seq", "hid"))
    per = slot_count // (columns * cores)
    rows = per * seq_count
    all_rows = slot_count * seq_count
    cfg = dict(hid=cores, seq=columns, seqs=seq_count, per=per, chunks=(4, 4, 2))

    outs = pl.pallas_call(
        functools.partial(local_kernel, cfg),
        out_shape=[jax.ShapeDtypeStruct((columns * rows, width + STAT), BF16)] * cores
        + [jax.ShapeDtypeStruct((slot_count, tok_count), F32)],
        in_specs=[HBM, HBM, HBM],
        out_specs=[VMEM] * (cores + 1),
        scratch_shapes=[
            pltpu.VMEM((tok_count, width), BF16),
            pltpu.VMEM((slot_count, width), BF16),
            pltpu.SMEM((1, seq_count), jnp.int32),
            pltpu.VMEM((all_rows, tok_count), BF16),
            pltpu.VMEM((all_rows, 1), F32),
            pltpu.VMEM((all_rows, 1), F32),
            pltpu.SemaphoreType.DMA((len(cfg["chunks"]),)),
            pltpu.SemaphoreType.DMA((2,)),
        ],
        compiler_params=params((tok_count * width, 2), (all_rows * tok_count, 4), (all_rows * width, 6)),
        name="local",
    )(far(seq_lengths), far(slot_embed.T), far(tokens))
    sums, logits = outs[:cores], outs[cores]

    chip = [sums[0]] + [swap(sums[u], "hid", u) for u in range(1, cores)]
    blocks = pl.pallas_call(
        functools.partial(chip_kernel, cores),
        out_shape=[jax.ShapeDtypeStruct((rows, width + STAT), BF16)] * columns,
        in_specs=[VMEM] * cores,
        out_specs=[VMEM] * columns,
        compiler_params=params((all_rows * width, 6)),
        name="chip",
    )(*chip)

    near_in = bring(blocks[0], w_in)
    got = [blocks[0]] + [cross(b, "seq", k) for k, b in zip(far_first(columns), blocks) if k]
    own = pl.pallas_call(
        column_kernel,
        out_shape=jax.ShapeDtypeStruct((rows, width), BF16),
        in_specs=[VMEM] * (columns + 1),
        out_specs=VMEM,
        compiler_params=params((all_rows * width, 6)),
        name="column",
    )(*got, near_in)

    near_out = bring(own, w_out)
    table = pl.pallas_call(
        functools.partial(table_kernel, cfg),
        out_shape=jax.ShapeDtypeStruct((tok_count, all_rows), BF16),
        in_specs=[SMEM, VMEM, VMEM],
        out_specs=VMEM,
        scratch_shapes=[
            pltpu.VMEM((slot_count, tok_count), F32),
            pltpu.VMEM((all_rows, tok_count), F32),
        ],
        compiler_params=params((all_rows * tok_count, 8)),
        cost_estimate=pl.CostEstimate(
            flops=8 * all_rows * tok_count,
            bytes_accessed=4 * all_rows * tok_count,
            transcendentals=slot_count * tok_count,
        ),
        name="table",
    )(seq_lengths, logits, own)

    spread = [reflect(own)] + [cross(own, "group", k) for k in range(1, groups)]
    parts = pl.pallas_call(
        functools.partial(expert_kernel, groups),
        out_shape=[jax.ShapeDtypeStruct((rows, width), BF16)] * groups,
        in_specs=[VMEM] * (groups + 3),
        out_specs=[VMEM] * groups,
        compiler_params=params((w_in.size, 2), (w_out.size, 2), (groups * rows * width, 6)),
        name="expert",
    )(*spread, near_in, near_out, table)
    back = [
        cross(part, "group", k if groups & (groups - 1) == 0 else groups - k)
        for k, part in zip(far_first(groups), parts)
        if k
    ] + [reflect(parts[0])]
    slot_rows = sum(b.astype(F32) for b in back).astype(BF16)

    column_rows = [slot_rows] + [cross(slot_rows, "seq", k) for k in range(1, columns)]
    every = list(column_rows)
    places = [u * columns + k for u in range(cores) for k in evens_first(columns)]
    for u in range(1, cores):
        every += [swap(r, "hid", u) for r in column_rows]

    return pl.pallas_call(
        functools.partial(mix_kernel, len(every), places),
        out_shape=jax.ShapeDtypeStruct((1, tok_count, width), BF16),
        in_specs=[VMEM] * (1 + len(every)),
        out_specs=HBM,
        scratch_shapes=[
            pltpu.VMEM((all_rows, width), BF16),
            pltpu.VMEM((tok_count, width), BF16),
            pltpu.SemaphoreType.DMA((9,)),
        ],
        compiler_params=params((all_rows * width, 4), (tok_count * width, 4)),
        name="mix",
    )(table, *[every[k] for k in places])


def solution(mesh):
    placed = (
        P("group", ("seq", "hid"), None),
        P(),
        P("group", None),
        P(("seq", "hid"), None, "group"),
        P(("seq", "hid"), "group", None),
    )
    return jax.shard_map(
        body,
        mesh=mesh,
        in_specs=placed,
        out_specs=P("group", ("seq", "hid"), None),
        check_vma=False,
    )
```

```python
import functools

import jax
import jax.numpy as jnp
from jax import lax
from jax.experimental import pallas as pl
from jax.experimental.pallas import tpu as pltpu
from jax.sharding import PartitionSpec as P


CHIP_VMEM = 67043328
EMPTY = -1e30
STAT = 128
BF16 = jnp.bfloat16
F32 = jnp.float32
VMEM = pl.BlockSpec(memory_space=pltpu.VMEM)
SMEM = pl.BlockSpec(memory_space=pltpu.SMEM)
HBM = pl.BlockSpec(memory_space=pltpu.HBM)


def params(*arrays):
    size = sum(2 * count * each for count, each in arrays)
    return pltpu.CompilerParams(vmem_limit_bytes=int(size) + (4 << 20))


def partner(index, step, size):
    if size & (size - 1) == 0:
        return index ^ step
    return (index + step) % size


def far_first(size):
    return [0] + list(range(size - 1, 0, -1))


def evens_first(size):
    return list(range(0, size, 2)) + list(range(1, size, 2))


def source(index, step, size):
    if size & (size - 1) == 0:
        return index ^ step
    return (index - step) % size


def cuts(count, shares):
    out, begin = [], 0
    for share in shares:
        size = count * share // sum(shares)
        out.append((begin, size))
        begin += size
    return out


def far(value):
    return pltpu.with_memory_space_constraint(value, pltpu.HBM)


def swap(value, axis, step):
    size = lax.axis_size(axis)
    return lax.ppermute(value, axis, [(i, partner(i, step, size)) for i in range(size)])


def mirror(core, cores):
    return cores - 1 - core


def cross(value, axis, step):
    size, cores = lax.axis_size(axis), lax.axis_size("hid")
    pairs = [
        (i * cores + c, partner(i, step, size) * cores + mirror(c, cores))
        for i in range(size)
        for c in range(cores)
    ]
    return lax.ppermute(value, (axis, "hid"), pairs)


def reflect(value):
    cores = lax.axis_size("hid")
    return lax.ppermute(value, "hid", [(c, mirror(c, cores)) for c in range(cores)])


def expert_of(column, core, step, cfg):
    return column * cfg["hid"] + (core if step else mirror(core, cfg["hid"]))


def split3(value):
    high = value.astype(BF16)
    rest = value - high.astype(F32)
    mid = rest.astype(BF16)
    low = (rest - mid.astype(F32)).astype(BF16)
    return high.astype(F32), mid.astype(F32), low.astype(F32)


def pack_stats(peak, total):
    rows = peak.shape[0]
    lane = lax.broadcasted_iota(jnp.int32, (rows, STAT), 1)
    out = jnp.zeros((rows, STAT), F32)
    for at, part in enumerate(split3(peak) + split3(total)):
        out = jnp.where(lane == at, part, out)
    return out.astype(BF16)


def read_stats(block):
    stats = block.astype(F32)
    lane = lax.broadcasted_iota(jnp.int32, stats.shape, 1)
    peak = jnp.sum(jnp.where(lane < 3, stats, 0.0), axis=1, keepdims=True)
    total = jnp.sum(jnp.where((lane >= 3) & (lane < 6), stats, 0.0), axis=1, keepdims=True)
    return peak, total


def member_mask(lengths_ref, offset, seq_count, tok_count):
    row = lax.broadcasted_iota(jnp.int32, (seq_count, tok_count), 0)
    place = offset + lax.broadcasted_iota(jnp.int32, (seq_count, tok_count), 1)
    begin = jnp.int32(0)
    starts = jnp.zeros((seq_count, tok_count), jnp.int32)
    ends = jnp.zeros((seq_count, tok_count), jnp.int32)
    for s in range(seq_count):
        end = begin + lengths_ref[0, s]
        starts = jnp.where(row == s, begin, starts)
        ends = jnp.where(row == s, end, ends)
        begin = end
    return (place >= starts) & (place < ends)


def place_of(cfg, tok_count):
    column, core = lax.axis_index("seq"), lax.axis_index("hid")
    return column, core, (column * cfg["hid"] + core) * tok_count


def local_kernel(cfg, lengths_hbm, embed_hbm, tok_hbm, *refs):
    outs, logits_ref = refs[: cfg["hid"]], refs[cfg["hid"]]
    (tok_ref, embed_ref, lengths_ref, weight_ref, peak_ref, total_ref, sems, small) = refs[
        cfg["hid"] + 1 :
    ]
    tok_count, width = tok_ref.shape
    seq_count, per = cfg["seqs"], cfg["per"]
    rows = per * seq_count
    get_embed = pltpu.make_async_copy(embed_hbm, embed_ref, small.at[0])
    get_embed.start()
    get_lengths = pltpu.make_async_copy(lengths_hbm, lengths_ref, small.at[1])
    get_lengths.start()
    copies = []
    pieces = cuts(width, cfg["chunks"])
    for i, (begin, size) in enumerate(pieces):
        part = pl.ds(begin, size)
        copy = pltpu.make_async_copy(tok_hbm.at[0, :, part], tok_ref.at[:, part], sems.at[i])
        copy.start()
        copies.append(copy)
    column, core, offset = place_of(cfg, tok_count)
    get_lengths.wait()
    mask = member_mask(lengths_ref, offset, seq_count, tok_count)
    get_embed.wait()
    for i, (begin, size) in enumerate(pieces):
        copies[i].wait()
        part = pl.ds(begin, size)
        more = lax.dot_general(
            embed_ref[:, part],
            tok_ref[:, part],
            (((1,), (1,)), ((), ())),
            preferred_element_type=F32,
        )
        logits_ref[...] = more if i == 0 else logits_ref[...] + more
    place = 0
    for u in range(cfg["hid"]):
        for k in range(cfg["seq"]):
            expert = expert_of(partner(column, k, cfg["seq"]), partner(core, u, cfg["hid"]), k, cfg)
            parts, peaks, totals = [], [], []
            for i in range(per):
                row = logits_ref[pl.ds(expert * per + i, 1), :]
                masked = jnp.where(mask, row, EMPTY)
                peak = jnp.max(masked, axis=1, keepdims=True)
                exponent = jnp.exp(masked - jnp.maximum(peak, EMPTY / 2))
                parts.append(exponent)
                peaks.append(peak)
                totals.append(jnp.sum(exponent, axis=1, keepdims=True))
            here = pl.ds(place * rows, rows)
            weight_ref[here, :] = jnp.concatenate(parts, axis=0).astype(BF16)
            peak_ref[here, :] = jnp.concatenate(peaks, axis=0)
            total_ref[here, :] = jnp.concatenate(totals, axis=0)
            place += 1
    each = cfg["seq"] * rows
    full = jnp.dot(weight_ref[...], tok_ref[...], preferred_element_type=F32)
    for u in range(cfg["hid"]):
        here = pl.ds(u * each, each)
        sums = full[u * each : (u + 1) * each]
        total = total_ref[here, :]
        outs[u][:, :width] = (sums * (1.0 / jnp.maximum(total, 1.0))).astype(BF16)
        outs[u][:, width:] = pack_stats(peak_ref[here, :], total)


def merge_blocks(blocks, width):
    stats = [read_stats(b[:, width:]) for b in blocks]
    peak = functools.reduce(jnp.maximum, [s[0] for s in stats])
    weights = [s[1] * jnp.exp(s[0] - peak) for s in stats]
    total = sum(weights)
    inverse = 1.0 / jnp.maximum(total, 1.0)
    merged = sum(b[:, :width].astype(F32) * (w * inverse) for b, w in zip(blocks, weights))
    return merged.astype(BF16), peak, total


def chip_kernel(count, *refs):
    ins, outs = refs[:count], refs[count:]
    rows, wide = outs[0].shape
    width = wide - STAT
    for k, out in zip(far_first(len(outs)), outs):
        here = slice(k * rows, (k + 1) * rows)
        merged, peak, total = merge_blocks([r[here, :] for r in ins], width)
        out[:, :width] = merged
        out[:, width:] = pack_stats(peak, total)


def column_kernel(*refs):
    ins, out = refs[:-2], refs[-1]
    merged, _, _ = merge_blocks([r[...] for r in ins], out.shape[1])
    out[...] = merged


def expert_kernel(count, *refs):
    ins, (w_in_ref, w_out_ref), outs = refs[:count], refs[count : count + 2], refs[count + 2 :]
    rows = ins[0].shape[0]
    picked = jnp.concatenate([r[...] for r in ins], axis=0)
    hidden = jax.nn.gelu(
        jnp.dot(picked, w_in_ref[0], preferred_element_type=F32), approximate=True
    ).astype(BF16)
    result = jnp.dot(hidden, w_out_ref[0], preferred_element_type=F32).astype(BF16)
    for k, out in zip(far_first(len(outs)), outs):
        out[...] = result[k * rows : (k + 1) * rows, :]


def table_kernel(cfg, lengths_ref, logits_ref, *refs):
    _, table_ref, mix_ref, wide_ref = refs
    slot_count, tok_count = logits_ref.shape
    seq_count, per = cfg["seqs"], cfg["per"]
    rows = per * seq_count
    logits = logits_ref[...]
    raised = jnp.exp(logits - jnp.max(logits, axis=0, keepdims=True))
    mix_ref[...] = raised / jnp.sum(raised, axis=0, keepdims=True)
    column, core, offset = place_of(cfg, tok_count)
    mask = member_mask(lengths_ref, offset, seq_count, tok_count)
    place = 0
    for u in range(cfg["hid"]):
        for k in range(cfg["seq"]):
            expert = expert_of(source(column, k, cfg["seq"]), source(core, u, cfg["hid"]), k, cfg)
            parts = [
                jnp.where(mask, mix_ref[pl.ds(expert * per + i, 1), :], 0.0) for i in range(per)
            ]
            wide_ref[pl.ds(place * rows, rows), :] = jnp.concatenate(parts, axis=0)
            place += 1
    table_ref[...] = jnp.transpose(wide_ref[...], (1, 0)).astype(BF16)


def load_kernel(_, far_ref, near_ref, sem):
    copy = pltpu.make_async_copy(far_ref, near_ref, sem)
    copy.start()
    copy.wait()


def bring(after, weights):
    return pl.pallas_call(
        load_kernel,
        out_shape=jax.ShapeDtypeStruct(weights.shape, BF16),
        in_specs=[VMEM, HBM],
        out_specs=VMEM,
        scratch_shapes=[pltpu.SemaphoreType.DMA],
        compiler_params=params((weights.size, 2)),
        cost_estimate=pl.CostEstimate(flops=0, bytes_accessed=4 * weights.size, transcendentals=0),
        name="load",
    )(after, far(weights))


def mix_kernel(count, places, table_ref, *refs):
    ins, out, held = refs[:count], refs[count], refs[count + 1]
    rows = ins[0].shape[0]
    done, sems = refs[count + 2 :]
    for k, r in zip(places, ins):
        held[k * rows : (k + 1) * rows, :] = r[...]
    steps = sems.shape[0] - 1
    tile = table_ref.shape[0] // steps
    copies = []
    ends = [tile // 2, tile] + [tile * k for k in range(2, steps)] + [tile * steps]
    begin = 0
    for i, end in enumerate(ends):
        part = pl.ds(begin, end - begin)
        begin = end
        done[part, :] = jnp.dot(table_ref[part, :], held[...], preferred_element_type=F32).astype(BF16)
        copy = pltpu.make_async_copy(done.at[part], out.at[0, part], sems.at[i])
        copy.start()
        copies.append(copy)
    for copy in copies:
        copy.wait()


def body(tokens, slot_embed, seq_lengths, w_in, w_out):
    _, tok_count, width = tokens.shape
    slot_count = slot_embed.shape[1]
    seq_count = seq_lengths.shape[1]
    groups, columns, cores = (lax.axis_size(a) for a in ("group", "seq", "hid"))
    per = slot_count // (columns * cores)
    rows = per * seq_count
    all_rows = slot_count * seq_count
    cfg = dict(hid=cores, seq=columns, seqs=seq_count, per=per, chunks=(4, 4, 2))

    outs = pl.pallas_call(
        functools.partial(local_kernel, cfg),
        out_shape=[jax.ShapeDtypeStruct((columns * rows, width + STAT), BF16)] * cores
        + [jax.ShapeDtypeStruct((slot_count, tok_count), F32)],
        in_specs=[HBM, HBM, HBM],
        out_specs=[VMEM] * (cores + 1),
        scratch_shapes=[
            pltpu.VMEM((tok_count, width), BF16),
            pltpu.VMEM((slot_count, width), BF16),
            pltpu.SMEM((1, seq_count), jnp.int32),
            pltpu.VMEM((all_rows, tok_count), BF16),
            pltpu.VMEM((all_rows, 1), F32),
            pltpu.VMEM((all_rows, 1), F32),
            pltpu.SemaphoreType.DMA((len(cfg["chunks"]),)),
            pltpu.SemaphoreType.DMA((2,)),
        ],
        compiler_params=params((tok_count * width, 2), (all_rows * tok_count, 4), (all_rows * width, 6)),
        name="local",
    )(far(seq_lengths), far(slot_embed.T), far(tokens))
    sums, logits = outs[:cores], outs[cores]

    chip = [sums[0]] + [swap(sums[u], "hid", u) for u in range(1, cores)]
    blocks = pl.pallas_call(
        functools.partial(chip_kernel, cores),
        out_shape=[jax.ShapeDtypeStruct((rows, width + STAT), BF16)] * columns,
        in_specs=[VMEM] * cores,
        out_specs=[VMEM] * columns,
        compiler_params=params((all_rows * width, 6)),
        name="chip",
    )(*chip)

    near_in = bring(blocks[0], w_in)
    got = [blocks[0]] + [cross(b, "seq", k) for k, b in zip(far_first(columns), blocks) if k]
    own = pl.pallas_call(
        column_kernel,
        out_shape=jax.ShapeDtypeStruct((rows, width), BF16),
        in_specs=[VMEM] * (columns + 1),
        out_specs=VMEM,
        compiler_params=params((all_rows * width, 6)),
        name="column",
    )(*got, near_in)

    near_out = bring(own, w_out)
    spread = [reflect(own)] + [cross(own, "group", k) for k in range(1, groups)]
    parts = pl.pallas_call(
        functools.partial(expert_kernel, groups),
        out_shape=[jax.ShapeDtypeStruct((rows, width), BF16)] * groups,
        in_specs=[VMEM] * (groups + 2),
        out_specs=[VMEM] * groups,
        compiler_params=params((w_in.size, 2), (w_out.size, 2), (groups * rows * width, 6)),
        name="expert",
    )(*spread, near_in, near_out)
    table = pl.pallas_call(
        functools.partial(table_kernel, cfg),
        out_shape=jax.ShapeDtypeStruct((tok_count, all_rows), BF16),
        in_specs=[SMEM, VMEM, VMEM],
        out_specs=VMEM,
        scratch_shapes=[
            pltpu.VMEM((slot_count, tok_count), F32),
            pltpu.VMEM((all_rows, tok_count), F32),
        ],
        compiler_params=params((all_rows * tok_count, 8)),
        cost_estimate=pl.CostEstimate(
            flops=8 * all_rows * tok_count,
            bytes_accessed=4 * all_rows * tok_count,
            transcendentals=slot_count * tok_count,
        ),
        name="table",
    )(seq_lengths, logits, parts[0])

    back = [
        cross(part, "group", k if groups & (groups - 1) == 0 else groups - k)
        for k, part in zip(far_first(groups), parts)
        if k
    ] + [reflect(parts[0])]
    slot_rows = sum(b.astype(F32) for b in back).astype(BF16)

    column_rows = [slot_rows] + [cross(slot_rows, "seq", k) for k in range(1, columns)]
    every = list(column_rows)
    places = [u * columns + k for u in range(cores) for k in evens_first(columns)]
    for u in range(1, cores):
        every += [swap(r, "hid", u) for r in column_rows]

    return pl.pallas_call(
        functools.partial(mix_kernel, len(every), places),
        out_shape=jax.ShapeDtypeStruct((1, tok_count, width), BF16),
        in_specs=[VMEM] * (1 + len(every)),
        out_specs=HBM,
        scratch_shapes=[
            pltpu.VMEM((all_rows, width), BF16),
            pltpu.VMEM((tok_count, width), BF16),
            pltpu.SemaphoreType.DMA((9,)),
        ],
        compiler_params=params((all_rows * width, 4), (tok_count * width, 4)),
        name="mix",
    )(table, *[every[k] for k in places])


def solution(mesh):
    placed = (
        P("group", ("seq", "hid"), None),
        P(),
        P("group", None),
        P(("seq", "hid"), None, "group"),
        P(("seq", "hid"), "group", None),
    )
    return jax.shard_map(
        body,
        mesh=mesh,
        in_specs=placed,
        out_specs=P("group", ("seq", "hid"), None),
        check_vma=False,
    )
```
